32 devices in a mesh: beam: 2 (over x), freq: 8 (over z, y), tm: 2 (over core).
Axes of the slice: x: 2, y: 2, z: 4, core: 2. Of those that a mesh axis runs over, the one named last changes fastest.
Arguments:
- spectra: float32 [4096, 5120], P(('beam', 'freq'), 'tm'), parts along dimension 0, may hold values from -6 to 6
- delays: int32 [11, 2048], replicated, may hold values from 0 to 1024, as said below
- widths: int32 [8], replicated, may hold values from 1 to 128, as said below
Outputs:
- filtered: float32 [8, 4096, 5120], P(None, ('beam', 'freq'), 'tm'), parts along dimension 1
The draws below stay inside these ranges and needn't reach their ends.
There are 2 independent parts, one for each index of `beam`. The reference program is written for one: setup_inputs(seed, part) draws one part's arguments, and reference() takes and returns one part's arrays. A program takes and returns all parts, laid end to end along the dimension named above; an argument that names none is the same for every part. Nothing has to cross between parts.
Inputs may be any that keep to these rules, and one draw needn't show every extreme that they name: delays[l, r] lies in 0 to 2 ** l, and every level l has some entry equal to 2 ** l. The widths include 1 and 128.
All inputs are finite; a program needn't handle non-finite values.
Results may differ from the reference program's by a relative error of at most 0.0003.
Values sent between devices are 32-bit elements; how exact they have to be, the bound alone decides.
A program may use at most 192 MiB of HBM per device.

```python
import jax
import jax.numpy as jnp
from jax import lax

F = 2048
LEVELS = 11
NW = 8
TAPS = 128
S = 5120


def draw_delays(key, part):
    draw_key, place_key = jax.random.split(jax.random.fold_in(key, 11))
    bounds = (2 ** jnp.arange(LEVELS)).astype(jnp.int32)
    delay_table = jax.random.randint(draw_key, (LEVELS, F), 0, bounds[:, None] + 1)
    column = jax.random.randint(place_key, (LEVELS,), 0, F)
    delay_table = delay_table.at[jnp.arange(LEVELS), column].set(bounds)
    return delay_table.astype(jnp.int32)


def draw_widths(key, part):
    draw_key, place_key = jax.random.split(jax.random.fold_in(key, 23))
    values = jax.random.randint(draw_key, (NW,), 2, TAPS)
    shuffled = jax.random.permutation(place_key, NW)
    values = values.at[shuffled[0]].set(1).at[shuffled[1]].set(TAPS)
    return values.astype(jnp.int32)


def block_levels(key, dims, cuts, low, high):
    loudness = 1.0
    for position, parts in cuts:
        steps = jax.random.uniform(jax.random.fold_in(jax.random.fold_in(key, 6), position), (parts,), jnp.float32, low / len(cuts), high / len(cuts))
        loudness = loudness * jnp.repeat(jnp.exp(steps), dims[position] // parts).reshape((-1,) + (1,) * (len(dims) - 1 - position))
    return loudness


def noise(own_key, extent, width, bound, cuts=(), kind=jnp.bfloat16):
    level = block_levels(own_key, extent, cuts, -0.22, 0.18) if cuts else 1.0
    drawn = jax.random.normal(own_key, extent, jnp.float32) * width * level
    return jnp.minimum(jnp.maximum(drawn, -bound), bound).astype(kind)


def setup_inputs(seed: int = 0, part: int = 0) -> dict:
    arg_keys = jax.random.split(jax.random.key(seed), 4)
    part_keys = jax.random.split(jax.random.fold_in(arg_keys[3], part), 4)
    return {
        "spectra": noise(part_keys[0], (F, S), 1.0, 6.0, ((0, 8), (1, 2)), jnp.float32),
        "delays": draw_delays(jax.random.fold_in(arg_keys[3], 71), part),
        "widths": draw_widths(jax.random.fold_in(arg_keys[3], 71), part),
    }


def delay_level(current, row_shifts, half_rows):
    row_count, out_width = current.shape
    group_count = row_count // (2 * half_rows)
    block_view = current.reshape(group_count, 2, half_rows, out_width)
    padded = jnp.pad(block_view[:, 1], ((0, 0), (0, 0), (0, half_rows)))
    source_rows = jnp.broadcast_to(padded[:, None], (group_count, 2, half_rows, out_width + half_rows))
    source_rows = source_rows.reshape(row_count, out_width + half_rows)
    delayed = jax.vmap(lambda row_data, offset_at: lax.dynamic_slice_in_dim(row_data, offset_at, out_width))(source_rows, row_shifts.astype(jnp.int32))
    summed = block_view[:, 0][:, None] + delayed.reshape(group_count, 2, half_rows, out_width)
    return summed.reshape(row_count, out_width)

def reference(spectra, delays, widths):
    current = spectra
    for tree_level in range(LEVELS):
        current = delay_level(current, delays[tree_level], 2 ** tree_level)
    padded = jnp.pad(current, ((0, 0), (1, TAPS)))
    running = jnp.cumsum(padded, axis=1)

    def filter_one(box_width):
        upper_sum = lax.dynamic_slice_in_dim(running, box_width.astype(jnp.int32), S, 1)
        scaling = 1.0 / jnp.sqrt(box_width.astype(jnp.float32) * F)
        return (upper_sum - running[:, :S]) * scaling
    return lax.map(filter_one, widths)
```

```python
import functools

import jax
import jax.numpy as jnp
from jax import lax
from jax.experimental import pallas as pl
from jax.experimental.pallas import tpu as pltpu
from jax.sharding import PartitionSpec as P

LANES = 128
SUB = 8
TAPS = 128
VMEM = pltpu.MemorySpace.VMEM
SMEM = pltpu.MemorySpace.SMEM
MESH = pl.DeviceIdType.MESH


def cdiv(a, b):
    return -(-a // b)


def round_up(a, b):
    return cdiv(a, b) * b


def shifted(src, start, width, shift, reach, lane):
    if reach >= LANES:
        start = start + lax.shift_right_logical(shift, LANES.bit_length() - 1)
        shift = shift & (LANES - 1)
    low = src[pl.ds(start, width), :]
    high = src[pl.ds(start + 1, width), :]
    return pltpu.roll(jnp.where(lane < shift, high, low), LANES - shift, 1)


class Plan:
    def __init__(self, rows, span, all_levels, all_rows, bands, halves, groups):
        self.rows, self.span = rows, span
        self.all_levels, self.all_rows = all_levels, all_rows
        self.levels = rows.bit_length() - 1
        self.bits = all_levels - self.levels
        self.bands, self.halves = bands, halves
        self.parts = bands * halves
        self.own = rows // self.parts
        self.groups = groups if self.own % (SUB * groups) == 0 else 1
        self.per = self.own // self.groups
        self.blocks = span // LANES
        self.lead_blocks = cdiv(rows - 1, LANES)
        self.blocks_a = SUB - self.lead_blocks
        self.blocks_b = self.blocks - self.blocks_a
        self.pitch_a = SUB
        self.pitch_b = round_up(self.blocks_b + self.lead_blocks, SUB)
        self.total = self.blocks * halves
        reach = 2 ** (all_levels - 1)
        self.pitch_x = round_up(self.total + cdiv(reach, LANES) + 2, SUB)
        self.out_blocks = self.blocks + 1


def tree_kernel(plan, delays, spectra, *refs):
    p = plan
    G, parts, halves, bands = p.groups, p.parts, p.halves, p.bands
    refs = list(refs)

    def take(n):
        got = refs[:n]
        del refs[:n]
        return got

    outs = take(G)
    (rows_in, lead) = take(2)
    tree_a, tree_b = take(2), take(2)
    (send_a,) = take(1)
    send_b = take(G)
    (came_a,) = take(1)
    came_b = take(G)
    ready = take(G)
    buf_a, buf_b = take(2)
    sems, own_sems, in_sems, lead_sems = take(4)

    beam, freq, tm = (lax.axis_index(n) for n in ("beam", "freq", "tm"))
    me = freq * halves + tm
    head = SUB * LANES

    load_a = pltpu.make_async_copy(spectra.at[:, :head], rows_in.at[:, :head], in_sems.at[0])
    load_b = pltpu.make_async_copy(spectra.at[:, head:], rows_in.at[:, head:], in_sems.at[1])
    load_a.start()
    load_b.start()

    def peer(k):
        other = me
        step = 1
        while step < parts:
            if k & step:
                other = other + step * (1 - 2 * ((me // step) % 2))
            step *= 2
        return other, (beam, other // halves, other % halves)

    barrier = pltpu.get_barrier_semaphore()
    for k in range(1, parts):
        pl.semaphore_signal(barrier, inc=1, device_id=peer(k)[1], device_id_type=MESH)

    def spread(buf, pitch, first, count, lead_count):
        def body(n, carry):
            at = pl.ds(pl.multiple_of(n * SUB, SUB), SUB)
            for b in range(count):
                v = rows_in[at, (first + b) * LANES : (first + b + 1) * LANES]
                buf[pl.ds(n * (SUB * pitch) + b, SUB, stride=pitch), :] = v
            for b in range(lead_count):
                v = lead[at, b * LANES : (b + 1) * LANES]
                v = jnp.where(tm < halves - 1, v, 0.0)
                buf[pl.ds(n * (SUB * pitch) + count + b, SUB, stride=pitch), :] = v
            return carry

        lax.fori_loop(0, p.rows // SUB, body, 0)

    mine = freq * p.rows

    def levels(bufs, pitch):
        lane = lax.broadcasted_iota(jnp.int32, (pitch, LANES), 1)
        src, dst = bufs
        for level in range(p.levels - 1):
            half = 2**level
            unroll = min(8, p.rows // 2)

            def pairs(n, carry, src=src, dst=dst, half=half, level=level):
                for u in range(unroll):
                    q = n * unroll + u
                    row_a = ((q >> level) << (level + 1)) + (q & (half - 1))
                    at_a = pl.multiple_of(row_a * pitch, SUB)
                    at_b = pl.multiple_of((row_a + half) * pitch, SUB)
                    a = src[pl.ds(at_a, pitch), :]
                    for e, at in enumerate((at_a, at_b)):
                        shift = delays[level, mine + row_a + e * half]
                        dst[pl.ds(at, pitch), :] = a + shifted(src, at_b, pitch, shift, half, lane)
                return carry

            lax.fori_loop(0, p.rows // 2 // unroll, pairs, 0)
            src, dst = dst, src
        return src

    def last_level(src, pitch, out, blocks, group, per):
        level = p.levels - 1
        half = 2**level
        per_bits, own_bits = per.bit_length() - 1, p.own.bit_length() - 1
        lane = lax.broadcasted_iota(jnp.int32, (blocks, LANES), 1)
        count = p.rows // 2 * per // p.own
        unroll = 8 if count % 8 == 0 else 1

        def last_pairs(n, carry):
            for u in range(unroll):
                m = n * unroll + u
                row_a = (m >> per_bits) * p.own + group * per + (m & (per - 1))
                at_a = pl.multiple_of(row_a * pitch, SUB)
                at_b = pl.multiple_of((row_a + half) * pitch, SUB)
                a = src[pl.ds(at_a, blocks), :]
                for e in range(2):
                    row = row_a + e * half
                    shift = delays[level, mine + row]
                    at = (m & (per - 1)) * blocks
                    out[row >> own_bits, pl.ds(at, blocks), :] = a + shifted(
                        src, at_b, blocks, shift, half, lane
                    )
            return carry

        lax.fori_loop(0, count // unroll, last_pairs, 0)

    def send(src, dst, turn):
        copies = []
        for k in range(parts - 1, 0, -1):
            other, where = peer(k)
            c = pltpu.make_async_remote_copy(
                src_ref=src.at[other],
                dst_ref=dst.at[me],
                send_sem=sems.at[0, turn, k],
                recv_sem=sems.at[1, turn, k],
                device_id=where,
                device_id_type=MESH,
            )
            c.start()
            copies.append(c)
        c = pltpu.make_async_copy(src.at[me], dst.at[me], own_sems.at[turn])
        c.start()
        return copies, c

    def arrive(sent):
        for c in sent[0]:
            c.wait_recv()
        sent[1].wait()

    load_a.wait()
    spread(tree_a[0], p.pitch_a, 0, min(SUB, p.blocks), 0)
    src = levels(tree_a, p.pitch_a)
    last_level(src, p.pitch_a, send_a, p.blocks_a, 0, p.own)

    pl.semaphore_wait(barrier, parts - 1)
    left = (tm + halves - 1) % halves
    get_lead = pltpu.make_async_remote_copy(
        src_ref=spectra.at[:, : p.lead_blocks * LANES],
        dst_ref=lead,
        send_sem=lead_sems.at[0],
        recv_sem=lead_sems.at[1],
        device_id=(beam, freq, left),
        device_id_type=MESH,
    )
    get_lead.start()
    sent_a = send(send_a, came_a, 0)

    load_b.wait()
    get_lead.wait()
    spread(tree_b[0], p.pitch_b, p.blocks_a, p.blocks_b, p.lead_blocks)
    src = levels(tree_b, p.pitch_b)
    sent_b = []
    for g in range(G):
        last_level(src, p.pitch_b, send_b[g], p.blocks_b, g, p.per)
        sent_b.append(send(send_b[g], came_b[g], 1 + g))

    total, pitch, rows = p.total, p.pitch_x, p.per
    lane = lax.broadcasted_iota(jnp.int32, (total, LANES), 1)
    out_lane = lax.broadcasted_iota(jnp.int32, (p.out_blocks, LANES), 1)
    zero = jnp.zeros((pitch - total, LANES), jnp.float32)

    def clear(r, carry):
        for buf in (buf_a, buf_b):
            buf[pl.ds(r * pitch + total, pitch - total), :] = zero
        return carry

    lax.fori_loop(0, bands * rows, clear, 0)
    for buf in (buf_a, buf_b):
        buf[pl.ds(bands * rows * pitch, SUB), :] = jnp.zeros((SUB, LANES), jnp.float32)

    back = []
    arrive(sent_a)
    for g in range(G):
        arrive(sent_b[g])

        def gather(i, carry, g=g):
            for s in range(bands):
                at = (s * rows + i) * pitch
                for c in range(halves):
                    piece = came_a[s * halves + c, pl.ds((g * rows + i) * p.blocks_a, p.blocks_a), :]
                    buf_a[pl.ds(at + c * p.blocks, p.blocks_a), :] = piece
                    piece = came_b[g][s * halves + c, pl.ds(i * p.blocks_b, p.blocks_b), :]
                    buf_a[pl.ds(at + c * p.blocks + p.blocks_a, p.blocks_b), :] = piece
            return carry

        lax.fori_loop(0, rows, gather, 0)

        src, dst = buf_a, buf_b
        for level in range(p.bits):
            step = 2**level
            reach = 2 ** (p.levels + level)

            def one_row(i, carry, src=src, dst=dst, step=step, level=level, reach=reach, g=g):
                for j in range(bands):
                    base = (j // (2 * step)) * (2 * step) + j % step
                    shift = delays[p.levels + level, j * p.rows + me * p.own + g * rows + i]
                    at_a = pl.multiple_of((base * rows + i) * pitch, SUB)
                    at_b = pl.multiple_of(((base + step) * rows + i) * pitch, SUB)
                    if level < p.bits - 1:
                        a = src[pl.ds(at_a, total), :]
                        at = pl.multiple_of((j * rows + i) * pitch, SUB)
                        dst[pl.ds(at, total), :] = a + shifted(src, at_b, total, shift, reach, lane)
                        continue
                    for c in range(halves):
                        a = src[pl.ds(at_a + c * p.blocks, p.out_blocks), :]
                        moved = shifted(src, at_b + c * p.blocks, p.out_blocks, shift, reach, out_lane)
                        ready[g][j * halves + c, pl.ds(i * p.out_blocks, p.out_blocks), :] = a + moved
                return carry

            lax.fori_loop(0, rows, one_row, 0)
            src, dst = dst, src
        back.append(send(ready[g], outs[g], 1 + G + g))
    for sent in back:
        arrive(sent)
    for sent in [sent_a] + sent_b + back:
        for c in sent[0]:
            c.wait_send()


def dedisperse(p, delays, spectra):
    G, parts = p.groups, p.parts
    out_shape = jax.ShapeDtypeStruct((parts, p.per * p.out_blocks, LANES), jnp.float32)
    here = pl.BlockSpec(memory_space=pl.ANY)
    f32 = jnp.float32
    turns = 1 + 2 * G
    return pl.pallas_call(
        functools.partial(tree_kernel, p),
        out_shape=[out_shape] * G,
        in_specs=[pl.BlockSpec(memory_space=SMEM), here],
        out_specs=[here] * G,
        scratch_shapes=[
            pltpu.VMEM((p.rows, p.span), f32),
            pltpu.VMEM((p.rows, p.lead_blocks * LANES), f32),
        ]
        + [pltpu.VMEM((p.rows * p.pitch_a + SUB, LANES), f32)] * 2
        + [pltpu.VMEM((p.rows * p.pitch_b + SUB, LANES), f32)] * 2
        + [pltpu.VMEM((parts, p.own * p.blocks_a, LANES), f32)]
        + [pltpu.VMEM((parts, p.per * p.blocks_b, LANES), f32)] * G
        + [pltpu.VMEM((parts, p.own * p.blocks_a, LANES), f32)]
        + [pltpu.VMEM((parts, p.per * p.blocks_b, LANES), f32)] * G
        + [pltpu.VMEM((parts, p.per * p.out_blocks, LANES), f32)] * G
        + [pltpu.VMEM((p.bands * p.per * p.pitch_x + SUB, LANES), f32)] * 2
        + [
            pltpu.SemaphoreType.DMA((2, turns, parts)),
            pltpu.SemaphoreType.DMA((turns,)),
            pltpu.SemaphoreType.DMA((2,)),
            pltpu.SemaphoreType.DMA((2,)),
        ],
        compiler_params=pltpu.CompilerParams(
            collective_id=0, has_side_effects=True, vmem_limit_bytes=40 << 20
        ),
    )(delays, spectra)


def filter_kernel(p, filters, parts, per_dot, widths, *refs):
    G = p.groups
    xs, (out, matrix, lhs) = refs[:G], refs[G:]
    rows = parts * p.per
    stride = p.out_blocks

    @pl.when(pl.program_id(0) == 0)
    def _():
        pos = lax.broadcasted_iota(jnp.int32, (2 * TAPS, TAPS), 0)
        dist = pos - lax.broadcasted_iota(jnp.int32, (2 * TAPS, TAPS), 1)
        for w in range(filters):
            box = (dist >= 0) & (dist < widths[w])
            value = jnp.where(box, 1.0, 0.0).astype(jnp.bfloat16)
            for n in range(2):
                matrix[n * 2 * TAPS : (n + 1) * 2 * TAPS, w * TAPS : (w + 1) * TAPS] = value

    for g, x in enumerate(xs):
        for n in range(p.blocks + 1):
            v = x[pl.ds(n, rows, stride=stride), :]
            h = v.astype(jnp.bfloat16)
            t = (v - h.astype(jnp.float32)).astype(jnp.bfloat16)
            for k, part in enumerate((h, h, t, t)):
                at = ((n - k % 2) * G + g) * rows
                if 0 <= n - k % 2 < p.blocks:
                    lhs[at : at + rows, k * LANES : (k + 1) * LANES] = part

    together = 2 if filters % 2 == 0 else 1
    for w in range(0, filters, together):
        m = matrix[:, w * TAPS : (w + together) * TAPS]
        scale = [
            1.0 / jnp.sqrt(jnp.full((SUB, LANES), widths[w + n], jnp.int32).astype(jnp.float32) * p.all_rows)
            for n in range(together)
        ]
        for first in range(0, p.blocks, per_dot):
            size = per_dot * G * rows
            y = jnp.dot(
                lhs[first * G * rows : first * G * rows + size, :], m, preferred_element_type=jnp.float32
            )
            for b in range(per_dot):
                at = (first + b) * LANES
                for g in range(G):
                    low = (b * G + g) * rows
                    for n in range(together):
                        part = y[low : low + rows, n * TAPS : (n + 1) * TAPS]
                        part = part * scale[n][:1]
                        shape = (out.shape[1], out.shape[2] // G, LANES)
                        out[w + n, :, g * shape[1] : (g + 1) * shape[1], at : at + LANES] = part.reshape(shape)


def filter_rows(p, xs, widths):
    filters = widths.shape[0]
    if p.per % SUB:
        parts, view = p.parts, (filters, 1, p.parts * p.own, p.span)
        block = view
    else:
        parts = 2 if p.parts % 2 == 0 else 1
        view = (filters, p.parts, p.own, p.span)
        block = (filters, parts, p.own, p.span)
    per_dot = 4 if p.blocks % 4 == 0 else 1
    rows = parts * p.per * p.out_blocks
    cells = filters * p.rows * p.span
    return pl.pallas_call(
        functools.partial(filter_kernel, p, filters, parts, per_dot),
        grid=(p.parts // parts,),
        out_shape=jax.ShapeDtypeStruct(view, jnp.float32),
        in_specs=[pl.BlockSpec(memory_space=SMEM)]
        + [pl.BlockSpec((rows, LANES), lambda s: (s, 0))] * p.groups,
        out_specs=pl.BlockSpec(block, lambda s: (0, s, 0, 0)),
        scratch_shapes=[
            pltpu.VMEM((4 * TAPS, filters * TAPS), jnp.bfloat16),
            pltpu.VMEM((p.blocks * p.groups * parts * p.per, 4 * TAPS), jnp.bfloat16),
        ],
        compiler_params=pltpu.CompilerParams(vmem_limit_bytes=40 << 20),
        cost_estimate=pl.CostEstimate(flops=1024 * cells, bytes_accessed=4 * cells, transcendentals=0),
    )(widths, *xs)


GROUPS = 2


def local(spectra, delays, widths):
    rows, span = spectra.shape
    p = Plan(rows, span, *delays.shape, lax.axis_size("freq"), lax.axis_size("tm"), GROUPS)
    xs = dedisperse(p, delays, spectra)
    xs = [x.reshape(-1, LANES) for x in xs]
    return filter_rows(p, xs, widths).reshape(widths.shape[0], rows, span)


def solution(mesh):
    return jax.shard_map(
        local,
        mesh=mesh,
        in_specs=(P(("beam", "freq"), "tm"), P(), P()),
        out_specs=P(None, ("beam", "freq"), "tm"),
        check_vma=False,
    )
```

```python
import functools

import jax
import jax.numpy as jnp
from jax import lax
from jax.experimental import pallas as pl
from jax.experimental.pallas import tpu as pltpu
from jax.sharding import PartitionSpec as P

LANES = 128
SUB = 8
VMEM = pltpu.MemorySpace.VMEM
SMEM = pltpu.MemorySpace.SMEM
MESH = pl.DeviceIdType.MESH


def cdiv(a, b):
    return -(-a // b)


def round_up(a, b):
    return cdiv(a, b) * b


def shifted(src, start, width, shift, lane):
    start = start + lax.shift_right_logical(shift, LANES.bit_length() - 1)
    shift = shift & (LANES - 1)
    low = src[pl.ds(start, width), :]
    high = src[pl.ds(start + 1, width), :]
    return pltpu.roll(jnp.where(lane < shift, high, low), LANES - shift, 1)


class Plan:
    def __init__(self, rows, span, all_levels, all_rows, bands, halves, groups):
        self.rows, self.span = rows, span
        self.all_levels, self.all_rows = all_levels, all_rows
        self.levels = rows.bit_length() - 1
        self.bits = all_levels - self.levels
        self.bands, self.halves = bands, halves
        self.parts = bands * halves
        self.own = rows // self.parts
        self.groups = groups if self.own % (SUB * groups) == 0 else 1
        self.per = self.own // self.groups
        self.blocks = span // LANES
        self.lead_blocks = cdiv(rows - 1, LANES)
        self.blocks_a = SUB - self.lead_blocks
        self.blocks_b = self.blocks - self.blocks_a
        self.pitch_a = SUB
        self.pitch_b = round_up(self.blocks_b + self.lead_blocks, SUB)
        self.total = self.blocks * halves
        reach = 2 ** (all_levels - 1)
        self.pitch_x = round_up(self.total + cdiv(reach, LANES) + 2, SUB)
        starts = list(range(0, self.levels, 3))
        self.passes = [(first, min(3, self.levels - first)) for first in starts]
        assert rows <= 2 * LANES and 2 ** self.passes[-1][0] >= self.own
        self.window = max(rows, LANES)


def tree_kernel(plan, delays, spectra, *refs):
    p = plan
    G, parts, halves, bands = p.groups, p.parts, p.halves, p.bands
    refs = list(refs)

    def take(n):
        got = refs[:n]
        del refs[:n]
        return got

    outs, edges = take(G), take(G)
    (rows_in, lead) = take(2)
    tree_a, tree_b = take(2), take(2)
    (send_a,) = take(1)
    send_b = take(G)
    (came_a,) = take(1)
    came_b = take(G)
    ready, ready_edge = take(G), take(G)
    buf_a, buf_b = take(2)
    own_delays, band_delays = take(2)
    sems, edge_sems, own_sems, in_sems, lead_sems, band_sems = take(6)

    beam, freq, tm = (lax.axis_index(n) for n in ("beam", "freq", "tm"))
    me = freq * halves + tm
    head = SUB * LANES

    load_a = pltpu.make_async_copy(spectra.at[:, :head], rows_in.at[:, :head], in_sems.at[0])
    load_b = pltpu.make_async_copy(spectra.at[:, head:], rows_in.at[:, head:], in_sems.at[1])
    own_first = freq * p.rows // p.window * p.window
    own_at = freq * p.rows - own_first
    load_own = pltpu.make_async_copy(
        delays.at[:, pl.ds(pl.multiple_of(own_first, LANES), p.window)], own_delays, in_sems.at[2]
    )
    load_bands = []
    for j in range(bands):
        at = (j * p.rows + me * p.own) // LANES * LANES
        load_bands.append(
            pltpu.make_async_copy(
                delays.at[:, pl.ds(pl.multiple_of(at, LANES), LANES)], band_delays.at[j], band_sems.at[j]
            )
        )
    load_a.start()
    load_own.start()
    load_b.start()
    for c in load_bands:
        c.start()

    def peer(k):
        other = me
        step = 1
        while step < parts:
            if k & step:
                other = other + step * (1 - 2 * ((me // step) % 2))
            step *= 2
        return other, (beam, other // halves, other % halves)

    barrier = pltpu.get_barrier_semaphore()
    for k in range(1, parts):
        pl.semaphore_signal(barrier, inc=1, device_id=peer(k)[1], device_id_type=MESH)

    def spread(buf, pitch, first, count, lead_count):
        def body(n, carry):
            at = pl.ds(pl.multiple_of(n * SUB, SUB), SUB)
            for b in range(count):
                v = rows_in[at, (first + b) * LANES : (first + b + 1) * LANES]
                buf[pl.ds(n * (SUB * pitch) + b, SUB, stride=pitch), :] = v
            for b in range(lead_count):
                v = lead[at, b * LANES : (b + 1) * LANES]
                v = jnp.where(tm < halves - 1, v, 0.0)
                buf[pl.ds(n * (SUB * pitch) + count + b, SUB, stride=pitch), :] = v
            return carry

        lax.fori_loop(0, p.rows // SUB, body, 0)

    def several(src, pitch, first, depth, base, put):
        lane = lax.broadcasted_iota(jnp.int32, (pitch, LANES), 1)
        half = 2**first
        rows = [src[pl.ds(pl.multiple_of((base + m * half) * pitch, SUB), pitch), :] for m in range(2**depth)]
        for t in range(depth):
            step = 2**t
            for m in range(2**depth):
                if m & step:
                    continue
                a, low = rows[m], rows[m + step]
                high = pltpu.roll(low, pitch - 1, 0)
                for q in (m, m + step):
                    shift = own_delays[first + t, own_at + base + q * half]
                    rows[q] = a + pltpu.roll(jnp.where(lane < shift, high, low), LANES - shift, 1)
        for m, v in enumerate(rows):
            put(base + m * half, v)

    def levels(bufs, pitch, together):
        src, dst = bufs
        for first, depth in p.passes[:-1]:
            count = p.rows >> depth

            def body(n, carry, src=src, dst=dst, first=first, depth=depth):
                def put(row, v):
                    dst[pl.ds(pl.multiple_of(row * pitch, SUB), pitch), :] = v

                for u in range(together):
                    q = n * together + u
                    base = ((q >> first) << (first + depth)) + (q & (2**first - 1))
                    several(src, pitch, first, depth, base, put)
                return carry

            lax.fori_loop(0, count // together, body, 0)
            src, dst = dst, src
        return src

    def last_levels(src, pitch, out, blocks, group, per, together):
        first, depth = p.passes[-1]
        per_bits, own_bits = per.bit_length() - 1, p.own.bit_length() - 1
        count = (p.rows >> depth) * per // p.own

        def body(n, carry):
            for u in range(together):
                q = n * together + u
                base = ((q >> per_bits) << own_bits) + group * per + (q & (per - 1))
                at = (q & (per - 1)) * blocks

                def put(row, v):
                    out[row >> own_bits, pl.ds(at, blocks), :] = v[:blocks]

                several(src, pitch, first, depth, base, put)
            return carry

        lax.fori_loop(0, count // together, body, 0)

    def send(src, dst, turn):
        copies = []
        for k in range(parts - 1, 0, -1):
            other, where = peer(k)
            c = pltpu.make_async_remote_copy(
                src_ref=src.at[other],
                dst_ref=dst.at[me],
                send_sem=sems.at[0, turn, k],
                recv_sem=sems.at[1, turn, k],
                device_id=where,
                device_id_type=MESH,
            )
            c.start()
            copies.append(c)
        c = pltpu.make_async_copy(src.at[me], dst.at[me], own_sems.at[turn])
        c.start()
        return copies, c

    def send_edges(src, dst, turn):
        copies = []
        for k in range(parts - 1, 0, -1):
            other, where = peer(k)
            c = pltpu.make_async_remote_copy(
                src_ref=src.at[other],
                dst_ref=dst.at[me],
                send_sem=edge_sems.at[0, turn, k],
                recv_sem=edge_sems.at[1, turn, k],
                device_id=where,
                device_id_type=MESH,
            )

            @pl.when(other % halves < halves - 1)
            def _(c=c):
                c.start()

            copies.append((other, c))
        c = pltpu.make_async_copy(src.at[me], dst.at[me], own_sems.at[1 + 2 * G + turn])

        @pl.when(tm < halves - 1)
        def _(c=c):
            c.start()

        return copies, c

    def arrive(sent):
        for c in sent[0]:
            c.wait_recv()
        sent[1].wait()

    load_a.wait()
    spread(tree_a[0], p.pitch_a, 0, SUB, 0)
    load_own.wait()
    src = levels(tree_a, p.pitch_a, 2)
    last_levels(src, p.pitch_a, send_a, p.blocks_a, 0, p.own, 2)

    pl.semaphore_wait(barrier, parts - 1)
    left = (tm + halves - 1) % halves
    get_lead = pltpu.make_async_remote_copy(
        src_ref=spectra.at[:, : p.lead_blocks * LANES],
        dst_ref=lead,
        send_sem=lead_sems.at[0],
        recv_sem=lead_sems.at[1],
        device_id=(beam, freq, left),
        device_id_type=MESH,
    )
    get_lead.start()
    sent_a = send(send_a, came_a, 0)

    load_b.wait()
    get_lead.wait()
    spread(tree_b[0], p.pitch_b, p.blocks_a, p.blocks_b, p.lead_blocks)
    src = levels(tree_b, p.pitch_b, 1)
    sent_b = []
    for g in range(G):
        last_levels(src, p.pitch_b, send_b[g], p.blocks_b, g, p.per, 1)
        sent_b.append(send(send_b[g], came_b[g], 1 + g))

    total, pitch, rows = p.total, p.pitch_x, p.per
    lane = lax.broadcasted_iota(jnp.int32, (total, LANES), 1)
    zero = jnp.zeros((pitch - total, LANES), jnp.float32)

    def clear(r, carry):
        for buf in (buf_a, buf_b):
            buf[pl.ds(r * pitch + total, pitch - total), :] = zero
        return carry

    lax.fori_loop(0, bands * rows, clear, 0)
    for buf in (buf_a, buf_b):
        buf[pl.ds(bands * rows * pitch, SUB), :] = jnp.zeros((SUB, LANES), jnp.float32)

    back, back_edges = [], []
    for c in load_bands:
        c.wait()
    arrive(sent_a)
    for g in range(G):
        arrive(sent_b[g])

        def gather(i, carry, g=g):
            for s in range(bands):
                at = (s * rows + i) * pitch
                for c in range(halves):
                    piece = came_a[s * halves + c, pl.ds((g * rows + i) * p.blocks_a, p.blocks_a), :]
                    buf_a[pl.ds(at + c * p.blocks, p.blocks_a), :] = piece
                    piece = came_b[g][s * halves + c, pl.ds(i * p.blocks_b, p.blocks_b), :]
                    buf_a[pl.ds(at + c * p.blocks + p.blocks_a, p.blocks_b), :] = piece
            return carry

        lax.fori_loop(0, rows, gather, 0)

        src, dst = buf_a, buf_b
        for level in range(p.bits):
            step = 2**level

            def one_row(i, carry, src=src, dst=dst, step=step, level=level, g=g):
                for j in range(bands):
                    base = (j // (2 * step)) * (2 * step) + j % step
                    at = (j * p.rows + me * p.own) % LANES + g * rows + i
                    shift = band_delays[j, p.levels + level, at]
                    at_a = pl.multiple_of((base * rows + i) * pitch, SUB)
                    at_b = pl.multiple_of(((base + step) * rows + i) * pitch, SUB)
                    if level < p.bits - 1:
                        a = src[pl.ds(at_a, total), :]
                        at = pl.multiple_of((j * rows + i) * pitch, SUB)
                        dst[pl.ds(at, total), :] = a + shifted(src, at_b, total, shift, lane)
                        continue
                    v = src[pl.ds(at_a, total), :] + shifted(src, at_b, total, shift, lane)
                    for c in range(halves):
                        first = c * p.blocks
                        ready[g][j * halves + c, pl.ds(i * p.blocks, p.blocks), :] = v[first : first + p.blocks]
                        if c > 0:
                            ready_edge[g][j * halves + c - 1, pl.ds(i, 1), :] = v[first : first + 1]
                return carry

            lax.fori_loop(0, rows, one_row, 0)
            src, dst = dst, src
        back.append(send(ready[g], outs[g], 1 + G + g))
        back_edges.append(send_edges(ready_edge[g], edges[g], g))
    for sent, (copies, c) in zip(back, back_edges):
        arrive(sent)

        @pl.when(tm < halves - 1)
        def _(copies=copies, c=c):
            for other, remote in copies:
                remote.wait_recv()
            c.wait()

    for sent in [sent_a] + sent_b + back:
        for c in sent[0]:
            c.wait_send()
    for copies, _ in back_edges:
        for other, remote in copies:

            @pl.when(other % halves < halves - 1)
            def _(remote=remote):
                remote.wait_send()


def dedisperse(p, delays, spectra):
    G, parts = p.groups, p.parts
    out_shape = jax.ShapeDtypeStruct((parts, p.per * p.blocks, LANES), jnp.float32)
    edge_shape = jax.ShapeDtypeStruct((parts, p.per, LANES), jnp.float32)
    here = pl.BlockSpec(memory_space=pl.ANY)
    f32 = jnp.float32
    turns = 1 + 2 * G
    return pl.pallas_call(
        functools.partial(tree_kernel, p),
        out_shape=[out_shape] * G + [edge_shape] * G,
        in_specs=[pl.BlockSpec(memory_space=pltpu.MemorySpace.HBM)] * 2,
        out_specs=[here] * (2 * G),
        scratch_shapes=[
            pltpu.VMEM((p.rows, p.span), f32),
            pltpu.VMEM((p.rows, p.lead_blocks * LANES), f32),
        ]
        + [pltpu.VMEM((p.rows * p.pitch_a + SUB, LANES), f32)] * 2
        + [pltpu.VMEM((p.rows * p.pitch_b + SUB, LANES), f32)] * 2
        + [pltpu.VMEM((parts, p.own * p.blocks_a, LANES), f32)]
        + [pltpu.VMEM((parts, p.per * p.blocks_b, LANES), f32)] * G
        + [pltpu.VMEM((parts, p.own * p.blocks_a, LANES), f32)]
        + [pltpu.VMEM((parts, p.per * p.blocks_b, LANES), f32)] * G
        + [pltpu.VMEM((parts, p.per * p.blocks, LANES), f32)] * G
        + [pltpu.VMEM((parts, p.per, LANES), f32)] * G
        + [pltpu.VMEM((p.bands * p.per * p.pitch_x + SUB, LANES), f32)] * 2
        + [
            pltpu.SMEM((p.all_levels, p.window), jnp.int32),
            pltpu.SMEM((p.bands, p.all_levels, LANES), jnp.int32),
            pltpu.SemaphoreType.DMA((2, turns, parts)),
            pltpu.SemaphoreType.DMA((2, G, parts)),
            pltpu.SemaphoreType.DMA((turns + G,)),
            pltpu.SemaphoreType.DMA((3,)),
            pltpu.SemaphoreType.DMA((2,)),
            pltpu.SemaphoreType.DMA((p.bands,)),
        ],
        compiler_params=pltpu.CompilerParams(
            collective_id=0, has_side_effects=True, vmem_limit_bytes=58 << 20
        ),
    )(delays, spectra)


def filter_kernel(p, filters, parts, widths, *refs):
    G = p.groups
    xs, edges, (out, matrix, lhs, sums) = refs[:G], refs[G : 2 * G], refs[2 * G :]
    rows = parts * p.per
    size = G * rows
    last = lax.axis_index("tm") == p.halves - 1

    @pl.when(pl.program_id(0) == 0)
    def _():
        source = lax.broadcasted_iota(jnp.int32, (LANES, LANES), 0)
        target = lax.broadcasted_iota(jnp.int32, (LANES, LANES), 1)
        for k, taken in enumerate((source <= target, source < LANES)):
            value = jnp.where(taken, 1.0, 0.0).astype(jnp.bfloat16)
            for n in range(2):
                matrix[n * LANES : (n + 1) * LANES, k * LANES : (k + 1) * LANES] = value

    for g in range(G):
        for n in range(p.blocks + 1):
            if n < p.blocks:
                v = xs[g][pl.ds(n, rows, stride=p.blocks), :]
            else:
                v = jnp.where(last, 0.0, edges[g][...])
            h = v.astype(jnp.bfloat16)
            t = (v - h.astype(jnp.float32)).astype(jnp.bfloat16)
            at = n * size + g * rows
            lhs[at : at + rows, :LANES] = h
            lhs[at : at + rows, LANES:] = t
    sums[...] = jnp.dot(lhs[...], matrix[...], preferred_element_type=jnp.float32)

    lane = lax.broadcasted_iota(jnp.int32, (size, LANES), 1)
    scale = []
    for w in range(filters):
        width = jnp.full((size, LANES), widths[w], jnp.int32).astype(jnp.float32)
        scale.append(1.0 / jnp.sqrt(width * p.all_rows))
    for n in range(p.blocks):
        here = slice(n * size, (n + 1) * size)
        low = sums[here, :LANES]
        high = sums[here, LANES:] + sums[(n + 1) * size : (n + 2) * size, :LANES]
        x = [xs[g][pl.ds(n, rows, stride=p.blocks), :] for g in range(G)]
        before = low - jnp.concatenate(x, axis=0)
        for w in range(filters):
            shift = widths[w] - 1
            upto = pltpu.roll(jnp.where(lane < shift, high, low), LANES - shift, 1)
            y = (upto - before) * scale[w]
            for g in range(G):
                shape = (out.shape[1], out.shape[2] // G, LANES)
                rows_out = slice(g * shape[1], (g + 1) * shape[1])
                out[w, :, rows_out, n * LANES : (n + 1) * LANES] = y[g * rows : (g + 1) * rows].reshape(shape)


def filter_rows(p, xs, edges, widths):
    filters = widths.shape[0]
    if p.per % SUB:
        parts, view = p.parts, (filters, 1, p.parts * p.own, p.span)
        block = view
    else:
        parts = PARTS if p.parts % PARTS == 0 else 1
        view = (filters, p.parts, p.own, p.span)
        block = (filters, parts, p.own, p.span)
    rows = parts * p.per
    total = rows * p.groups * (p.blocks + 1)
    cells = filters * p.rows * p.span
    return pl.pallas_call(
        functools.partial(filter_kernel, p, filters, parts),
        grid=(p.parts // parts,),
        out_shape=jax.ShapeDtypeStruct(view, jnp.float32),
        in_specs=[pl.BlockSpec(memory_space=SMEM)]
        + [pl.BlockSpec((rows * p.blocks, LANES), lambda s: (s, 0))] * p.groups
        + [pl.BlockSpec((rows, LANES), lambda s: (s, 0))] * p.groups,
        out_specs=pl.BlockSpec(block, lambda s: (0, s, 0, 0)),
        scratch_shapes=[
            pltpu.VMEM((2 * LANES, 2 * LANES), jnp.bfloat16),
            pltpu.VMEM((total, 2 * LANES), jnp.bfloat16),
            pltpu.VMEM((total, 2 * LANES), jnp.float32),
        ],
        compiler_params=pltpu.CompilerParams(vmem_limit_bytes=58 << 20),
        cost_estimate=pl.CostEstimate(flops=96 * cells, bytes_accessed=4 * cells, transcendentals=0),
    )(widths, *xs, *edges)


PARTS = 4
GROUPS = 2


def local(spectra, delays, widths):
    rows, span = spectra.shape
    p = Plan(rows, span, *delays.shape, lax.axis_size("freq"), lax.axis_size("tm"), GROUPS)
    made = [x.reshape(-1, LANES) for x in dedisperse(p, delays, spectra)]
    out = filter_rows(p, made[: p.groups], made[p.groups :], widths)
    return out.reshape(widths.shape[0], rows, span)


def solution(mesh):
    return jax.shard_map(
        local,
        mesh=mesh,
        in_specs=(P(("beam", "freq"), "tm"), P(), P()),
        out_specs=P(None, ("beam", "freq"), "tm"),
        check_vma=False,
    )
```

```python
import functools

import jax
import jax.numpy as jnp
from jax import lax
from jax.experimental import pallas as pl
from jax.experimental.pallas import tpu as pltpu
from jax.sharding import PartitionSpec as P

LANES = 128
SUB = 8
VMEM = pltpu.MemorySpace.VMEM
SMEM = pltpu.MemorySpace.SMEM
MESH = pl.DeviceIdType.MESH


def cdiv(a, b):
    return -(-a // b)


def round_up(a, b):
    return cdiv(a, b) * b


def shifted(src, start, width, shift, lane):
    start = start + lax.shift_right_logical(shift, LANES.bit_length() - 1)
    shift = shift & (LANES - 1)
    low = src[pl.ds(start, width), :]
    high = src[pl.ds(start + 1, width), :]
    return pltpu.roll(jnp.where(lane < shift, high, low), LANES - shift, 1)


class Plan:
    def __init__(self, rows, span, all_levels, all_rows, bands, halves, groups):
        self.rows, self.span = rows, span
        self.all_levels, self.all_rows = all_levels, all_rows
        self.levels = rows.bit_length() - 1
        self.bits = all_levels - self.levels
        self.bands, self.halves = bands, halves
        self.parts = bands * halves
        self.own = rows // self.parts
        self.groups = groups if self.own % (SUB * groups) == 0 else 1
        self.per = self.own // self.groups
        self.blocks = span // LANES
        self.lead_blocks = cdiv(rows - 1, LANES)
        self.blocks_a = SUB - self.lead_blocks
        self.blocks_b = self.blocks - self.blocks_a
        self.pitch_a = SUB
        self.pitch_b = round_up(self.blocks_b + self.lead_blocks, SUB)
        self.total = self.blocks * halves
        reach = 2 ** (all_levels - 1)
        self.pitch_x = round_up(self.total + cdiv(reach, LANES) + 2, SUB)
        starts = list(range(0, self.levels, 3))
        self.passes = [(first, min(3, self.levels - first)) for first in starts]
        assert rows <= 2 * LANES and 2 ** self.passes[-1][0] >= self.own
        self.window = max(rows, LANES)


def tree_kernel(plan, delays, spectra, *refs):
    p = plan
    G, parts, halves, bands = p.groups, p.parts, p.halves, p.bands
    refs = list(refs)

    def take(n):
        got = refs[:n]
        del refs[:n]
        return got

    outs, edges = take(G), take(G)
    (rows_in, lead) = take(2)
    tree_a, tree_b = take(2), take(2)
    (send_a,) = take(1)
    send_b = take(G)
    (came_a,) = take(1)
    came_b = take(G)
    ready, ready_edge = take(G), take(G)
    buf_a, buf_b = take(2)
    own_delays, band_delays = take(2)
    sems, edge_sems, own_sems, in_sems, lead_sems, band_sems = take(6)

    beam, freq, tm = (lax.axis_index(n) for n in ("beam", "freq", "tm"))
    me = freq * halves + tm
    head = SUB * LANES

    load_a = pltpu.make_async_copy(spectra.at[:, :head], rows_in.at[:, :head], in_sems.at[0])
    load_b = pltpu.make_async_copy(spectra.at[:, head:], rows_in.at[:, head:], in_sems.at[1])
    own_first = freq * p.rows // p.window * p.window
    own_at = freq * p.rows - own_first
    load_own = pltpu.make_async_copy(
        delays.at[:, pl.ds(pl.multiple_of(own_first, LANES), p.window)], own_delays, in_sems.at[2]
    )
    load_bands = []
    for j in range(bands):
        at = (j * p.rows + me * p.own) // LANES * LANES
        load_bands.append(
            pltpu.make_async_copy(
                delays.at[:, pl.ds(pl.multiple_of(at, LANES), LANES)], band_delays.at[j], band_sems.at[j]
            )
        )
    load_a.start()
    load_own.start()
    load_b.start()
    for c in load_bands:
        c.start()

    def peer(k):
        other = me
        step = 1
        while step < parts:
            if k & step:
                other = other + step * (1 - 2 * ((me // step) % 2))
            step *= 2
        return other, (beam, other // halves, other % halves)

    barrier = pltpu.get_barrier_semaphore()
    for k in range(1, parts):
        pl.semaphore_signal(barrier, inc=1, device_id=peer(k)[1], device_id_type=MESH)

    def spread(buf, pitch, first, count, lead_count):
        def body(n, carry):
            at = pl.ds(pl.multiple_of(n * SUB, SUB), SUB)
            for b in range(count):
                v = rows_in[at, (first + b) * LANES : (first + b + 1) * LANES]
                buf[pl.ds(n * (SUB * pitch) + b, SUB, stride=pitch), :] = v
            for b in range(lead_count):
                v = lead[at, b * LANES : (b + 1) * LANES]
                v = jnp.where(tm < halves - 1, v, 0.0)
                buf[pl.ds(n * (SUB * pitch) + count + b, SUB, stride=pitch), :] = v
            return carry

        lax.fori_loop(0, p.rows // SUB, body, 0)

    def several(src, pitch, first, depth, base, put):
        lane = lax.broadcasted_iota(jnp.int32, (pitch, LANES), 1)
        half = 2**first
        rows = [src[pl.ds(pl.multiple_of((base + m * half) * pitch, SUB), pitch), :] for m in range(2**depth)]
        for t in range(depth):
            step = 2**t
            for m in range(2**depth):
                if m & step:
                    continue
                a, low = rows[m], rows[m + step]
                high = pltpu.roll(low, pitch - 1, 0)
                for q in (m, m + step):
                    shift = own_delays[first + t, own_at + base + q * half]
                    rows[q] = a + pltpu.roll(jnp.where(lane < shift, high, low), LANES - shift, 1)
        for m, v in enumerate(rows):
            put(base + m * half, v)

    def levels(bufs, pitch, together):
        src, dst = bufs
        for first, depth in p.passes[:-1]:
            count = p.rows >> depth
            unroll = min(together, count)

            def body(n, carry, src=src, dst=dst, first=first, depth=depth, unroll=unroll):
                def put(row, v):
                    dst[pl.ds(pl.multiple_of(row * pitch, SUB), pitch), :] = v

                for u in range(unroll):
                    q = n * unroll + u
                    base = ((q >> first) << (first + depth)) + (q & (2**first - 1))
                    several(src, pitch, first, depth, base, put)
                return carry

            lax.fori_loop(0, count // unroll, body, 0)
            src, dst = dst, src
        return src

    def last_levels(src, pitch, out, blocks, group, per, together):
        first, depth = p.passes[-1]
        per_bits, own_bits = per.bit_length() - 1, p.own.bit_length() - 1
        count = (p.rows >> depth) * per // p.own
        unroll = min(together, count)

        def body(n, carry):
            for u in range(unroll):
                q = n * unroll + u
                base = ((q >> per_bits) << own_bits) + group * per + (q & (per - 1))
                at = (q & (per - 1)) * blocks

                def put(row, v):
                    out[row >> own_bits, pl.ds(at, blocks), :] = v[:blocks]

                several(src, pitch, first, depth, base, put)
            return carry

        lax.fori_loop(0, count // unroll, body, 0)

    def send(src, dst, turn):
        copies = []
        for k in range(parts - 1, 0, -1):
            other, where = peer(k)
            c = pltpu.make_async_remote_copy(
                src_ref=src.at[other],
                dst_ref=dst.at[me],
                send_sem=sems.at[0, turn, k],
                recv_sem=sems.at[1, turn, k],
                device_id=where,
                device_id_type=MESH,
            )
            c.start()
            copies.append(c)
        c = pltpu.make_async_copy(src.at[me], dst.at[me], own_sems.at[turn])
        c.start()
        return copies, c

    def send_edges(src, dst, turn):
        copies = []
        for k in range(parts - 1, 0, -1):
            other, where = peer(k)
            c = pltpu.make_async_remote_copy(
                src_ref=src.at[other],
                dst_ref=dst.at[me],
                send_sem=edge_sems.at[0, turn, k],
                recv_sem=edge_sems.at[1, turn, k],
                device_id=where,
                device_id_type=MESH,
            )

            @pl.when(other % halves < halves - 1)
            def _(c=c):
                c.start()

            copies.append((other, c))
        c = pltpu.make_async_copy(src.at[me], dst.at[me], own_sems.at[1 + 2 * G + turn])

        @pl.when(tm < halves - 1)
        def _(c=c):
            c.start()

        return copies, c

    def arrive(sent):
        for c in sent[0]:
            c.wait_recv()
        sent[1].wait()

    load_a.wait()
    spread(tree_a[0], p.pitch_a, 0, SUB, 0)
    load_own.wait()
    src = levels(tree_a, p.pitch_a, 8)
    last_levels(src, p.pitch_a, send_a, p.blocks_a, 0, p.own, 8)

    pl.semaphore_wait(barrier, parts - 1)
    left = (tm + halves - 1) % halves
    get_lead = pltpu.make_async_remote_copy(
        src_ref=spectra.at[:, : p.lead_blocks * LANES],
        dst_ref=lead,
        send_sem=lead_sems.at[0],
        recv_sem=lead_sems.at[1],
        device_id=(beam, freq, left),
        device_id_type=MESH,
    )
    get_lead.start()
    sent_a = send(send_a, came_a, 0)

    load_b.wait()
    get_lead.wait()
    spread(tree_b[0], p.pitch_b, p.blocks_a, p.blocks_b, p.lead_blocks)
    src = levels(tree_b, p.pitch_b, 4)
    sent_b = []
    for g in range(G):
        last_levels(src, p.pitch_b, send_b[g], p.blocks_b, g, p.per, 4)
        sent_b.append(send(send_b[g], came_b[g], 1 + g))

    total, pitch, rows = p.total, p.pitch_x, p.per
    lane = lax.broadcasted_iota(jnp.int32, (total, LANES), 1)
    zero = jnp.zeros((pitch - total, LANES), jnp.float32)

    def clear(r, carry):
        for buf in (buf_a, buf_b):
            buf[pl.ds(r * pitch + total, pitch - total), :] = zero
        return carry

    lax.fori_loop(0, bands * rows, clear, 0)
    for buf in (buf_a, buf_b):
        buf[pl.ds(bands * rows * pitch, SUB), :] = jnp.zeros((SUB, LANES), jnp.float32)

    back, back_edges = [], []
    for c in load_bands:
        c.wait()
    arrive(sent_a)
    for g in range(G):
        arrive(sent_b[g])

        def gather(i, carry, g=g):
            for s in range(bands):
                at = (s * rows + i) * pitch
                for c in range(halves):
                    piece = came_a[s * halves + c, pl.ds((g * rows + i) * p.blocks_a, p.blocks_a), :]
                    buf_a[pl.ds(at + c * p.blocks, p.blocks_a), :] = piece
                    piece = came_b[g][s * halves + c, pl.ds(i * p.blocks_b, p.blocks_b), :]
                    buf_a[pl.ds(at + c * p.blocks + p.blocks_a, p.blocks_b), :] = piece
            return carry

        lax.fori_loop(0, rows, gather, 0)

        src, dst = buf_a, buf_b
        for level in range(p.bits):
            step = 2**level

            def one_row(i, carry, src=src, dst=dst, step=step, level=level, g=g):
                for j in range(bands):
                    base = (j // (2 * step)) * (2 * step) + j % step
                    at = (j * p.rows + me * p.own) % LANES + g * rows + i
                    shift = band_delays[j, p.levels + level, at]
                    at_a = pl.multiple_of((base * rows + i) * pitch, SUB)
                    at_b = pl.multiple_of(((base + step) * rows + i) * pitch, SUB)
                    if level < p.bits - 1:
                        a = src[pl.ds(at_a, total), :]
                        at = pl.multiple_of((j * rows + i) * pitch, SUB)
                        dst[pl.ds(at, total), :] = a + shifted(src, at_b, total, shift, lane)
                        continue
                    v = src[pl.ds(at_a, total), :] + shifted(src, at_b, total, shift, lane)
                    for c in range(halves):
                        first = c * p.blocks
                        ready[g][j * halves + c, pl.ds(i * p.blocks, p.blocks), :] = v[first : first + p.blocks]
                        if c > 0:
                            ready_edge[g][j * halves + c - 1, pl.ds(i, 1), :] = v[first : first + 1]
                return carry

            lax.fori_loop(0, rows, one_row, 0)
            src, dst = dst, src
        back.append(send(ready[g], outs[g], 1 + G + g))
        back_edges.append(send_edges(ready_edge[g], edges[g], g))
    for sent, (copies, c) in zip(back, back_edges):
        arrive(sent)

        @pl.when(tm < halves - 1)
        def _(copies=copies, c=c):
            for other, remote in copies:
                remote.wait_recv()
            c.wait()

    for sent in [sent_a] + sent_b + back:
        for c in sent[0]:
            c.wait_send()
    for copies, _ in back_edges:
        for other, remote in copies:

            @pl.when(other % halves < halves - 1)
            def _(remote=remote):
                remote.wait_send()


def dedisperse(p, delays, spectra):
    G, parts = p.groups, p.parts
    out_shape = jax.ShapeDtypeStruct((parts, p.per * p.blocks, LANES), jnp.float32)
    edge_shape = jax.ShapeDtypeStruct((parts, p.per, LANES), jnp.float32)
    here = pl.BlockSpec(memory_space=pl.ANY)
    f32 = jnp.float32
    turns = 1 + 2 * G
    return pl.pallas_call(
        functools.partial(tree_kernel, p),
        out_shape=[out_shape] * G + [edge_shape] * G,
        in_specs=[pl.BlockSpec(memory_space=pltpu.MemorySpace.HBM)] * 2,
        out_specs=[here] * (2 * G),
        scratch_shapes=[
            pltpu.VMEM((p.rows, p.span), f32),
            pltpu.VMEM((p.rows, p.lead_blocks * LANES), f32),
        ]
        + [pltpu.VMEM((p.rows * p.pitch_a + SUB, LANES), f32)] * 2
        + [pltpu.VMEM((p.rows * p.pitch_b + SUB, LANES), f32)] * 2
        + [pltpu.VMEM((parts, p.own * p.blocks_a, LANES), f32)]
        + [pltpu.VMEM((parts, p.per * p.blocks_b, LANES), f32)] * G
        + [pltpu.VMEM((parts, p.own * p.blocks_a, LANES), f32)]
        + [pltpu.VMEM((parts, p.per * p.blocks_b, LANES), f32)] * G
        + [pltpu.VMEM((parts, p.per * p.blocks, LANES), f32)] * G
        + [pltpu.VMEM((parts, p.per, LANES), f32)] * G
        + [pltpu.VMEM((p.bands * p.per * p.pitch_x + SUB, LANES), f32)] * 2
        + [
            pltpu.SMEM((p.all_levels, p.window), jnp.int32),
            pltpu.SMEM((p.bands, p.all_levels, LANES), jnp.int32),
            pltpu.SemaphoreType.DMA((2, turns, parts)),
            pltpu.SemaphoreType.DMA((2, G, parts)),
            pltpu.SemaphoreType.DMA((turns + G,)),
            pltpu.SemaphoreType.DMA((3,)),
            pltpu.SemaphoreType.DMA((2,)),
            pltpu.SemaphoreType.DMA((p.bands,)),
        ],
        compiler_params=pltpu.CompilerParams(
            collective_id=0, has_side_effects=True, vmem_limit_bytes=58 << 20
        ),
    )(delays, spectra)


def filter_kernel(p, filters, parts, widths, *refs):
    G = p.groups
    xs, edges, (out, matrix, lhs, sums) = refs[:G], refs[G : 2 * G], refs[2 * G :]
    rows = parts * p.per
    size = G * rows
    last = lax.axis_index("tm") == p.halves - 1

    @pl.when(pl.program_id(0) == 0)
    def _():
        source = lax.broadcasted_iota(jnp.int32, (LANES, LANES), 0)
        target = lax.broadcasted_iota(jnp.int32, (LANES, LANES), 1)
        for k, taken in enumerate((source <= target, source < LANES)):
            value = jnp.where(taken, 1.0, 0.0).astype(jnp.bfloat16)
            for n in range(2):
                matrix[n * LANES : (n + 1) * LANES, k * LANES : (k + 1) * LANES] = value

    for g in range(G):
        for n in range(p.blocks + 1):
            if n < p.blocks:
                v = xs[g][pl.ds(n, rows, stride=p.blocks), :]
            else:
                v = jnp.where(last, 0.0, edges[g][...])
            h = v.astype(jnp.bfloat16)
            t = (v - h.astype(jnp.float32)).astype(jnp.bfloat16)
            at = n * size + g * rows
            lhs[at : at + rows, :LANES] = h
            lhs[at : at + rows, LANES:] = t
    sums[...] = jnp.dot(lhs[...], matrix[...], preferred_element_type=jnp.float32)

    lane = lax.broadcasted_iota(jnp.int32, (size, LANES), 1)
    scale = []
    for w in range(filters):
        width = jnp.full((size, LANES), widths[w], jnp.int32).astype(jnp.float32)
        scale.append(1.0 / jnp.sqrt(width * p.all_rows))
    for n in range(p.blocks):
        here = slice(n * size, (n + 1) * size)
        low = sums[here, :LANES]
        high = sums[here, LANES:] + sums[(n + 1) * size : (n + 2) * size, :LANES]
        x = [xs[g][pl.ds(n, rows, stride=p.blocks), :] for g in range(G)]
        before = low - jnp.concatenate(x, axis=0)
        for w in range(filters):
            shift = widths[w] - 1
            upto = pltpu.roll(jnp.where(lane < shift, high, low), LANES - shift, 1)
            y = (upto - before) * scale[w]
            for g in range(G):
                shape = (out.shape[1], out.shape[2] // G, LANES)
                rows_out = slice(g * shape[1], (g + 1) * shape[1])
                out[w, :, rows_out, n * LANES : (n + 1) * LANES] = y[g * rows : (g + 1) * rows].reshape(shape)


def filter_rows(p, xs, edges, widths):
    filters = widths.shape[0]
    if p.per % SUB:
        parts, view = p.parts, (filters, 1, p.parts * p.own, p.span)
        block = view
    else:
        parts = PARTS if p.parts % PARTS == 0 else 1
        view = (filters, p.parts, p.own, p.span)
        block = (filters, parts, p.own, p.span)
    rows = parts * p.per
    total = rows * p.groups * (p.blocks + 1)
    cells = filters * p.rows * p.span
    return pl.pallas_call(
        functools.partial(filter_kernel, p, filters, parts),
        grid=(p.parts // parts,),
        out_shape=jax.ShapeDtypeStruct(view, jnp.float32),
        in_specs=[pl.BlockSpec(memory_space=SMEM)]
        + [pl.BlockSpec((rows * p.blocks, LANES), lambda s: (s, 0))] * p.groups
        + [pl.BlockSpec((rows, LANES), lambda s: (s, 0))] * p.groups,
        out_specs=pl.BlockSpec(block, lambda s: (0, s, 0, 0)),
        scratch_shapes=[
            pltpu.VMEM((2 * LANES, 2 * LANES), jnp.bfloat16),
            pltpu.VMEM((total, 2 * LANES), jnp.bfloat16),
            pltpu.VMEM((total, 2 * LANES), jnp.float32),
        ],
        compiler_params=pltpu.CompilerParams(vmem_limit_bytes=58 << 20),
        cost_estimate=pl.CostEstimate(flops=96 * cells, bytes_accessed=4 * cells, transcendentals=0),
    )(widths, *xs, *edges)


PARTS = 4
GROUPS = 2


def local(spectra, delays, widths):
    rows, span = spectra.shape
    p = Plan(rows, span, *delays.shape, lax.axis_size("freq"), lax.axis_size("tm"), GROUPS)
    made = [x.reshape(-1, LANES) for x in dedisperse(p, delays, spectra)]
    out = filter_rows(p, made[: p.groups], made[p.groups :], widths)
    return out.reshape(widths.shape[0], rows, span)


def solution(mesh):
    return jax.shard_map(
        local,
        mesh=mesh,
        in_specs=(P(("beam", "freq"), "tm"), P(), P()),
        out_specs=P(None, ("beam", "freq"), "tm"),
        check_vma=False,
    )
```

```python
import functools

import jax
import jax.numpy as jnp
from jax import lax
from jax.experimental import pallas as pl
from jax.experimental.pallas import tpu as pltpu
from jax.sharding import PartitionSpec as P

LANES = 128
SUB = 8
VMEM = pltpu.MemorySpace.VMEM
SMEM = pltpu.MemorySpace.SMEM
MESH = pl.DeviceIdType.MESH


def cdiv(a, b):
    return -(-a // b)


def round_up(a, b):
    return cdiv(a, b) * b


def shifted(src, start, width, shift, lane):
    start = start + lax.shift_right_logical(shift, LANES.bit_length() - 1)
    shift = shift & (LANES - 1)
    low = src[pl.ds(start, width), :]
    high = src[pl.ds(start + 1, width), :]
    return pltpu.roll(jnp.where(lane < shift, high, low), LANES - shift, 1)


def flipped(me, k, parts):
    other = me
    step = 1
    while step < parts:
        if k & step:
            other = other + step * (1 - 2 * ((me // step) % 2))
        step *= 2
    return other


class Plan:
    def __init__(self, rows, span, all_levels, all_rows, bands, halves, groups):
        self.rows, self.span = rows, span
        self.all_levels, self.all_rows = all_levels, all_rows
        self.levels = rows.bit_length() - 1
        self.bits = all_levels - self.levels
        self.bands, self.halves = bands, halves
        self.parts = bands * halves
        self.own = rows // self.parts
        self.groups = groups if self.own % (SUB * groups) == 0 else 1
        self.per = self.own // self.groups
        self.blocks = span // LANES
        self.lead_blocks = cdiv(rows - 1, LANES)
        self.blocks_a = SUB - self.lead_blocks
        self.blocks_b = self.blocks - self.blocks_a
        self.pitch_a = SUB
        self.pitch_b = round_up(self.blocks_b + self.lead_blocks, SUB)
        self.total = self.blocks * halves
        reach = 2 ** (all_levels - 1)
        self.pitch_x = round_up(self.total + cdiv(reach, LANES) + 2, SUB)
        self.relays = RELAYS if self.groups > 1 and self.parts >= 2 * RELAYS else 0
        self.far = self.parts // 2
        starts = list(range(0, self.levels, 3))
        self.passes = [(first, min(3, self.levels - first)) for first in starts]
        assert rows <= 2 * LANES and 2 ** self.passes[-1][0] >= self.own
        self.window = max(rows, LANES)


def tree_kernel(plan, delays, spectra, *refs):
    p = plan
    G, parts, halves, bands = p.groups, p.parts, p.halves, p.bands
    refs = list(refs)

    def take(n):
        got = refs[:n]
        del refs[:n]
        return got

    outs, edges = take(G), take(G)
    relay = take(1)[0] if p.relays else None
    (rows_in, lead) = take(2)
    tree_a, tree_b = take(2), take(2)
    (send_a,) = take(1)
    send_b = take(G)
    (came_a,) = take(1)
    came_b = take(G)
    ready, ready_edge = take(G), take(G)
    buf_a, buf_b = take(2)
    own_delays, band_delays = take(2)
    sems, edge_sems, own_sems, in_sems, lead_sems, band_sems, relay_sems = take(7)

    beam, freq, tm = (lax.axis_index(n) for n in ("beam", "freq", "tm"))
    me = freq * halves + tm
    head = SUB * LANES

    load_a = pltpu.make_async_copy(spectra.at[:, :head], rows_in.at[:, :head], in_sems.at[0])
    load_b = pltpu.make_async_copy(spectra.at[:, head:], rows_in.at[:, head:], in_sems.at[1])
    own_first = freq * p.rows // p.window * p.window
    own_at = freq * p.rows - own_first
    load_own = pltpu.make_async_copy(
        delays.at[:, pl.ds(pl.multiple_of(own_first, LANES), p.window)], own_delays, in_sems.at[2]
    )
    load_bands = []
    for j in range(bands):
        at = (j * p.rows + me * p.own) // LANES * LANES
        load_bands.append(
            pltpu.make_async_copy(
                delays.at[:, pl.ds(pl.multiple_of(at, LANES), LANES)], band_delays.at[j], band_sems.at[j]
            )
        )
    load_a.start()
    load_own.start()
    load_b.start()
    for c in load_bands:
        c.start()

    def peer(k):
        other = flipped(me, k, parts)
        return other, (beam, other // halves, other % halves)

    barrier = pltpu.get_barrier_semaphore()
    for k in range(1, parts):
        pl.semaphore_signal(barrier, inc=1, device_id=peer(k)[1], device_id_type=MESH)

    def spread(buf, pitch, first, count, lead_count):
        def body(n, carry):
            at = pl.ds(pl.multiple_of(n * SUB, SUB), SUB)
            for b in range(count):
                v = rows_in[at, (first + b) * LANES : (first + b + 1) * LANES]
                buf[pl.ds(n * (SUB * pitch) + b, SUB, stride=pitch), :] = v
            for b in range(lead_count):
                v = lead[at, b * LANES : (b + 1) * LANES]
                v = jnp.where(tm < halves - 1, v, 0.0)
                buf[pl.ds(n * (SUB * pitch) + count + b, SUB, stride=pitch), :] = v
            return carry

        lax.fori_loop(0, p.rows // SUB, body, 0)

    def several(src, pitch, first, depth, base, put):
        lane = lax.broadcasted_iota(jnp.int32, (pitch, LANES), 1)
        half = 2**first
        rows = [src[pl.ds(pl.multiple_of((base + m * half) * pitch, SUB), pitch), :] for m in range(2**depth)]
        for t in range(depth):
            step = 2**t
            for m in range(2**depth):
                if m & step:
                    continue
                a, low = rows[m], rows[m + step]
                high = pltpu.roll(low, pitch - 1, 0)
                for q in (m, m + step):
                    shift = own_delays[first + t, own_at + base + q * half]
                    rows[q] = a + pltpu.roll(jnp.where(lane < shift, high, low), LANES - shift, 1)
        for m, v in enumerate(rows):
            put(base + m * half, v)

    def levels(bufs, pitch, together):
        src, dst = bufs
        for first, depth in p.passes[:-1]:
            count = p.rows >> depth
            unroll = min(together, count)

            def body(n, carry, src=src, dst=dst, first=first, depth=depth, unroll=unroll):
                def put(row, v):
                    dst[pl.ds(pl.multiple_of(row * pitch, SUB), pitch), :] = v

                for u in range(unroll):
                    q = n * unroll + u
                    base = ((q >> first) << (first + depth)) + (q & (2**first - 1))
                    several(src, pitch, first, depth, base, put)
                return carry

            lax.fori_loop(0, count // unroll, body, 0)
            src, dst = dst, src
        return src

    def last_levels(src, pitch, out, blocks, group, per, together):
        first, depth = p.passes[-1]
        per_bits, own_bits = per.bit_length() - 1, p.own.bit_length() - 1
        count = (p.rows >> depth) * per // p.own
        unroll = min(together, count)

        def body(n, carry):
            for u in range(unroll):
                q = n * unroll + u
                base = ((q >> per_bits) << own_bits) + group * per + (q & (per - 1))
                at = (q & (per - 1)) * blocks

                def put(row, v):
                    out[row >> own_bits, pl.ds(at, blocks), :] = v[:blocks]

                several(src, pitch, first, depth, base, put)
            return carry

        lax.fori_loop(0, count // unroll, body, 0)

    def send(src, dst, turn, left_out=()):
        copies = []
        for k in range(parts - 1, 0, -1):
            if k in left_out:
                continue
            other, where = peer(k)
            c = pltpu.make_async_remote_copy(
                src_ref=src.at[other],
                dst_ref=dst.at[me],
                send_sem=sems.at[0, turn, k],
                recv_sem=sems.at[1, turn, k],
                device_id=where,
                device_id_type=MESH,
            )
            c.start()
            copies.append(c)
        c = pltpu.make_async_copy(src.at[me], dst.at[me], own_sems.at[turn])
        c.start()
        return copies, c

    def send_edges(src, dst, turn, left_out=()):
        copies = []
        for k in range(parts - 1, 0, -1):
            if k in left_out:
                continue
            other, where = peer(k)
            c = pltpu.make_async_remote_copy(
                src_ref=src.at[other],
                dst_ref=dst.at[me],
                send_sem=edge_sems.at[0, turn, k],
                recv_sem=edge_sems.at[1, turn, k],
                device_id=where,
                device_id_type=MESH,
            )

            @pl.when(other % halves < halves - 1)
            def _(c=c):
                c.start()

            copies.append((other, c))
        c = pltpu.make_async_copy(src.at[me], dst.at[me], own_sems.at[1 + 2 * G + turn])

        @pl.when(tm < halves - 1)
        def _(c=c):
            c.start()

        return copies, c

    def send_relays(src, src_edge):
        copies = []
        for k in range(p.relays):
            other, _ = peer(p.far + k)
            for n, (x, first, size) in enumerate(((src, 0, p.per * p.blocks), (src_edge, p.per * p.blocks, p.per))):
                to = relay.at[k, pl.ds(first, size)]
                if k == 0:
                    c = pltpu.make_async_copy(x.at[other], to, relay_sems.at[0, n, k])
                else:
                    c = pltpu.make_async_remote_copy(
                        src_ref=x.at[other],
                        dst_ref=to,
                        send_sem=relay_sems.at[0, n, k],
                        recv_sem=relay_sems.at[1, n, k],
                        device_id=peer(k)[1],
                        device_id_type=MESH,
                    )
                c.start()
                copies.append(c)
        return copies

    def arrive(sent):
        for c in sent[0]:
            c.wait_recv()
        sent[1].wait()

    load_a.wait()
    spread(tree_a[0], p.pitch_a, 0, SUB, 0)
    load_own.wait()
    src = levels(tree_a, p.pitch_a, 8)
    last_levels(src, p.pitch_a, send_a, p.blocks_a, 0, p.own, 8)

    pl.semaphore_wait(barrier, parts - 1)
    left = (tm + halves - 1) % halves
    get_lead = pltpu.make_async_remote_copy(
        src_ref=spectra.at[:, : p.lead_blocks * LANES],
        dst_ref=lead,
        send_sem=lead_sems.at[0],
        recv_sem=lead_sems.at[1],
        device_id=(beam, freq, left),
        device_id_type=MESH,
    )
    get_lead.start()
    sent_a = send(send_a, came_a, 0)

    load_b.wait()
    get_lead.wait()
    spread(tree_b[0], p.pitch_b, p.blocks_a, p.blocks_b, p.lead_blocks)
    src = levels(tree_b, p.pitch_b, 4)
    sent_b = []
    for g in range(G):
        last_levels(src, p.pitch_b, send_b[g], p.blocks_b, g, p.per, 4)
        sent_b.append(send(send_b[g], came_b[g], 1 + g))

    total, pitch, rows = p.total, p.pitch_x, p.per
    lane = lax.broadcasted_iota(jnp.int32, (total, LANES), 1)
    zero = jnp.zeros((pitch - total, LANES), jnp.float32)

    def clear(r, carry):
        for buf in (buf_a, buf_b):
            buf[pl.ds(r * pitch + total, pitch - total), :] = zero
        return carry

    lax.fori_loop(0, bands * rows, clear, 0)
    for buf in (buf_a, buf_b):
        buf[pl.ds(bands * rows * pitch, SUB), :] = jnp.zeros((SUB, LANES), jnp.float32)

    back, back_edges = [], []
    for c in load_bands:
        c.wait()
    arrive(sent_a)
    for g in range(G):
        arrive(sent_b[g])

        def gather(i, carry, g=g):
            for s in range(bands):
                at = (s * rows + i) * pitch
                for c in range(halves):
                    piece = came_a[s * halves + c, pl.ds((g * rows + i) * p.blocks_a, p.blocks_a), :]
                    buf_a[pl.ds(at + c * p.blocks, p.blocks_a), :] = piece
                    piece = came_b[g][s * halves + c, pl.ds(i * p.blocks_b, p.blocks_b), :]
                    buf_a[pl.ds(at + c * p.blocks + p.blocks_a, p.blocks_b), :] = piece
            return carry

        lax.fori_loop(0, rows, gather, 0)

        src, dst = buf_a, buf_b
        for level in range(p.bits):
            step = 2**level

            def one_row(i, carry, src=src, dst=dst, step=step, level=level, g=g):
                for j in range(bands):
                    base = (j // (2 * step)) * (2 * step) + j % step
                    at = (j * p.rows + me * p.own) % LANES + g * rows + i
                    shift = band_delays[j, p.levels + level, at]
                    at_a = pl.multiple_of((base * rows + i) * pitch, SUB)
                    at_b = pl.multiple_of(((base + step) * rows + i) * pitch, SUB)
                    if level < p.bits - 1:
                        a = src[pl.ds(at_a, total), :]
                        at = pl.multiple_of((j * rows + i) * pitch, SUB)
                        dst[pl.ds(at, total), :] = a + shifted(src, at_b, total, shift, lane)
                        continue
                    v = src[pl.ds(at_a, total), :] + shifted(src, at_b, total, shift, lane)
                    for c in range(halves):
                        first = c * p.blocks
                        ready[g][j * halves + c, pl.ds(i * p.blocks, p.blocks), :] = v[first : first + p.blocks]
                        if c > 0:
                            ready_edge[g][j * halves + c - 1, pl.ds(i, 1), :] = v[first : first + 1]
                return carry

            lax.fori_loop(0, rows, one_row, 0)
            src, dst = dst, src
        left_out = range(p.far, p.far + p.relays) if g == G - 1 else ()
        back.append(send(ready[g], outs[g], 1 + G + g, left_out))
        back_edges.append(send_edges(ready_edge[g], edges[g], g, left_out))
    relayed = send_relays(ready[G - 1], ready_edge[G - 1])
    for sent, (copies, c) in zip(back, back_edges):
        arrive(sent)

        @pl.when(tm < halves - 1)
        def _(copies=copies, c=c):
            for other, remote in copies:
                remote.wait_recv()
            c.wait()

    for c in relayed:
        c.wait()
    for sent in [sent_a] + sent_b + back:
        for c in sent[0]:
            c.wait_send()
    for copies, _ in back_edges:
        for other, remote in copies:

            @pl.when(other % halves < halves - 1)
            def _(remote=remote):
                remote.wait_send()


def dedisperse(p, delays, spectra):
    G, parts = p.groups, p.parts
    out_shape = jax.ShapeDtypeStruct((parts, p.per * p.blocks, LANES), jnp.float32)
    edge_shape = jax.ShapeDtypeStruct((parts, p.per, LANES), jnp.float32)
    relay_shapes = []
    if p.relays:
        relay_shapes = [jax.ShapeDtypeStruct((p.relays, p.per * (p.blocks + 1), LANES), jnp.float32)]
    here = pl.BlockSpec(memory_space=pl.ANY)
    f32 = jnp.float32
    turns = 1 + 2 * G
    return pl.pallas_call(
        functools.partial(tree_kernel, p),
        out_shape=[out_shape] * G + [edge_shape] * G + relay_shapes,
        in_specs=[pl.BlockSpec(memory_space=pltpu.MemorySpace.HBM)] * 2,
        out_specs=[here] * (2 * G + len(relay_shapes)),
        scratch_shapes=[
            pltpu.VMEM((p.rows, p.span), f32),
            pltpu.VMEM((p.rows, p.lead_blocks * LANES), f32),
        ]
        + [pltpu.VMEM((p.rows * p.pitch_a + SUB, LANES), f32)] * 2
        + [pltpu.VMEM((p.rows * p.pitch_b + SUB, LANES), f32)] * 2
        + [pltpu.VMEM((parts, p.own * p.blocks_a, LANES), f32)]
        + [pltpu.VMEM((parts, p.per * p.blocks_b, LANES), f32)] * G
        + [pltpu.VMEM((parts, p.own * p.blocks_a, LANES), f32)]
        + [pltpu.VMEM((parts, p.per * p.blocks_b, LANES), f32)] * G
        + [pltpu.VMEM((parts, p.per * p.blocks, LANES), f32)] * G
        + [pltpu.VMEM((parts, p.per, LANES), f32)] * G
        + [pltpu.VMEM((p.bands * p.per * p.pitch_x + SUB, LANES), f32)] * 2
        + [
            pltpu.SMEM((p.all_levels, p.window), jnp.int32),
            pltpu.SMEM((p.bands, p.all_levels, LANES), jnp.int32),
            pltpu.SemaphoreType.DMA((2, turns, parts)),
            pltpu.SemaphoreType.DMA((2, G, parts)),
            pltpu.SemaphoreType.DMA((turns + G,)),
            pltpu.SemaphoreType.DMA((3,)),
            pltpu.SemaphoreType.DMA((2,)),
            pltpu.SemaphoreType.DMA((p.bands,)),
            pltpu.SemaphoreType.DMA((2, 2, max(p.relays, 1))),
        ],
        compiler_params=pltpu.CompilerParams(
            collective_id=0, has_side_effects=True, vmem_limit_bytes=58 << 20
        ),
    )(delays, spectra)


def fill_matrix(matrix):
    source = lax.broadcasted_iota(jnp.int32, (LANES, LANES), 0)
    target = lax.broadcasted_iota(jnp.int32, (LANES, LANES), 1)
    for k, taken in enumerate((source <= target, source < LANES)):
        value = jnp.where(taken, 1.0, 0.0).astype(jnp.bfloat16)
        for n in range(2):
            matrix[n * LANES : (n + 1) * LANES, k * LANES : (k + 1) * LANES] = value


def prefix_sums(blocks, size, get, matrix, lhs, sums):
    for n in range(blocks + 1):
        v = get(n)
        h = v.astype(jnp.bfloat16)
        t = (v - h.astype(jnp.float32)).astype(jnp.bfloat16)
        lhs[n * size : (n + 1) * size, :LANES] = h
        lhs[n * size : (n + 1) * size, LANES:] = t
    sums[...] = jnp.dot(lhs[...], matrix[...], preferred_element_type=jnp.float32)


def box_ends(n, size, get, sums):
    low = sums[n * size : (n + 1) * size, :LANES]
    high = sums[n * size : (n + 1) * size, LANES:] + sums[(n + 1) * size : (n + 2) * size, :LANES]
    return low, high, low - get(n)


def box_scale(width, all_rows, shape):
    return 1.0 / jnp.sqrt(jnp.full(shape, width, jnp.int32).astype(jnp.float32) * all_rows)


def box(ends, width, scale, lane):
    low, high, before = ends
    shift = width - 1
    upto = pltpu.roll(jnp.where(lane < shift, high, low), LANES - shift, 1)
    return (upto - before) * scale


def filter_kernel(p, filters, parts, widths, *refs):
    G = p.groups
    xs, edges, (out, matrix, lhs, sums) = refs[:G], refs[G : 2 * G], refs[2 * G :]
    rows = parts * p.per
    size = G * rows
    last = lax.axis_index("tm") == p.halves - 1

    @pl.when(pl.program_id(0) == 0)
    def _():
        fill_matrix(matrix)

    def get(n):
        if n < p.blocks:
            return jnp.concatenate([x[pl.ds(n, rows, stride=p.blocks), :] for x in xs], axis=0)
        return jnp.where(last, 0.0, jnp.concatenate([e[...] for e in edges], axis=0))

    prefix_sums(p.blocks, size, get, matrix, lhs, sums)
    lane = lax.broadcasted_iota(jnp.int32, (size, LANES), 1)
    scale = [box_scale(widths[w], p.all_rows, (size, LANES)) for w in range(filters)]
    for n in range(p.blocks):
        ends = box_ends(n, size, get, sums)
        for w in range(filters):
            y = box(ends, widths[w], scale[w], lane)
            for g in range(G):
                shape = (out.shape[1], out.shape[2] // G, LANES)
                rows_out = slice(g * shape[1], (g + 1) * shape[1])
                out[w, :, rows_out, n * LANES : (n + 1) * LANES] = y[g * rows : (g + 1) * rows].reshape(shape)


def late_kernel(p, filters, widths, x, filtered, out, made, matrix, lhs, sums, sems):
    size = p.relays * p.per
    halves = p.halves
    tm = lax.axis_index("tm")
    me = lax.axis_index("freq") * halves + tm
    fill_matrix(matrix)
    stride = p.per * (p.blocks + 1)

    def get(n):
        pieces = []
        for k in range(p.relays):
            if n < p.blocks:
                v = x[pl.ds(k * stride + n, p.per, stride=p.blocks), :]
            else:
                v = jnp.where(tm == halves - 1, 0.0, x[pl.ds(k * stride + p.per * p.blocks, p.per), :])
            pieces.append(v)
        return jnp.concatenate(pieces, axis=0)

    prefix_sums(p.blocks, size, get, matrix, lhs, sums)
    lane = lax.broadcasted_iota(jnp.int32, (size, LANES), 1)
    copies = []
    for w in range(filters):
        scale = box_scale(widths[w], p.all_rows, (size, LANES))
        for n in range(p.blocks):
            y = box(box_ends(n, size, get, sums), widths[w], scale, lane)
            for k in range(p.relays):
                made[w, k, :, n * LANES : (n + 1) * LANES] = y[k * p.per : (k + 1) * p.per]
        for k in range(p.relays):
            part = flipped(me, p.far + k, p.parts)
            at = out.at[w, part, pl.ds((p.groups - 1) * p.per, p.per)]
            c = pltpu.make_async_copy(made.at[w, k], at, sems.at[w, k])
            c.start()
            copies.append(c)
    for c in copies:
        c.wait()


def filter_late(p, x, filtered, widths):
    filters = widths.shape[0]
    size = p.relays * p.per
    total = size * (p.blocks + 1)
    cells = filters * size * p.span
    return pl.pallas_call(
        functools.partial(late_kernel, p, filters),
        out_shape=jax.ShapeDtypeStruct(filtered.shape, jnp.float32),
        in_specs=[
            pl.BlockSpec(memory_space=SMEM),
            pl.BlockSpec(memory_space=VMEM),
            pl.BlockSpec(memory_space=pl.ANY),
        ],
        out_specs=pl.BlockSpec(memory_space=pl.ANY),
        scratch_shapes=[
            pltpu.VMEM((filters, p.relays, p.per, p.span), jnp.float32),
            pltpu.VMEM((2 * LANES, 2 * LANES), jnp.bfloat16),
            pltpu.VMEM((total, 2 * LANES), jnp.bfloat16),
            pltpu.VMEM((total, 2 * LANES), jnp.float32),
            pltpu.SemaphoreType.DMA((filters, p.relays)),
        ],
        input_output_aliases={2: 0},
        compiler_params=pltpu.CompilerParams(vmem_limit_bytes=32 << 20),
        cost_estimate=pl.CostEstimate(flops=96 * cells, bytes_accessed=4 * cells, transcendentals=0),
    )(widths, x, filtered)


def filter_rows(p, xs, edges, widths):
    filters = widths.shape[0]
    if p.per % SUB:
        parts, view = p.parts, (filters, 1, p.parts * p.own, p.span)
        block = view
    else:
        parts = PARTS if p.parts % PARTS == 0 else 1
        view = (filters, p.parts, p.own, p.span)
        block = (filters, parts, p.own, p.span)
    rows = parts * p.per
    total = rows * p.groups * (p.blocks + 1)
    cells = filters * p.rows * p.span
    return pl.pallas_call(
        functools.partial(filter_kernel, p, filters, parts),
        grid=(p.parts // parts,),
        out_shape=jax.ShapeDtypeStruct(view, jnp.float32),
        in_specs=[pl.BlockSpec(memory_space=SMEM)]
        + [pl.BlockSpec((rows * p.blocks, LANES), lambda s: (s, 0))] * p.groups
        + [pl.BlockSpec((rows, LANES), lambda s: (s, 0))] * p.groups,
        out_specs=pl.BlockSpec(block, lambda s: (0, s, 0, 0)),
        scratch_shapes=[
            pltpu.VMEM((2 * LANES, 2 * LANES), jnp.bfloat16),
            pltpu.VMEM((total, 2 * LANES), jnp.bfloat16),
            pltpu.VMEM((total, 2 * LANES), jnp.float32),
        ],
        compiler_params=pltpu.CompilerParams(vmem_limit_bytes=58 << 20),
        cost_estimate=pl.CostEstimate(flops=96 * cells, bytes_accessed=4 * cells, transcendentals=0),
    )(widths, *xs, *edges)


PARTS = 4
RELAYS = 4
GROUPS = 2


def local(spectra, delays, widths):
    rows, span = spectra.shape
    p = Plan(rows, span, *delays.shape, lax.axis_size("freq"), lax.axis_size("tm"), GROUPS)
    made = [x.reshape(-1, LANES) for x in dedisperse(p, delays, spectra)]
    xs, edges, relay = made[: p.groups], made[p.groups : 2 * p.groups], made[2 * p.groups :]
    if relay:
        swap = [(f, (f + p.bands // 2) % p.bands) for f in range(p.bands)]
        late = lax.ppermute(relay[0], "freq", swap)
    out = filter_rows(p, xs, edges, widths)
    if relay:
        out = filter_late(p, late, out, widths)
    return out.reshape(widths.shape[0], rows, span)


def solution(mesh):
    return jax.shard_map(
        local,
        mesh=mesh,
        in_specs=(P(("beam", "freq"), "tm"), P(), P()),
        out_specs=P(None, ("beam", "freq"), "tm"),
        check_vma=False,
    )
```

```python
import functools

import jax
import jax.numpy as jnp
from jax import lax
from jax.experimental import pallas as pl
from jax.experimental.pallas import tpu as pltpu
from jax.sharding import PartitionSpec as P

LANES = 128
SUB = 8
VMEM = pltpu.MemorySpace.VMEM
SMEM = pltpu.MemorySpace.SMEM
MESH = pl.DeviceIdType.MESH


def cdiv(a, b):
    return -(-a // b)


def round_up(a, b):
    return cdiv(a, b) * b


def shifted(src, start, width, shift, lane):
    start = start + lax.shift_right_logical(shift, LANES.bit_length() - 1)
    shift = shift & (LANES - 1)
    low = src[pl.ds(start, width), :]
    high = src[pl.ds(start + 1, width), :]
    return pltpu.roll(jnp.where(lane < shift, high, low), LANES - shift, 1)


def flipped(me, k, parts):
    other = me
    step = 1
    while step < parts:
        if k & step:
            other = other + step * (1 - 2 * ((me // step) % 2))
        step *= 2
    return other


class Plan:
    def __init__(self, rows, span, all_levels, all_rows, bands, halves, groups):
        self.rows, self.span = rows, span
        self.all_levels, self.all_rows = all_levels, all_rows
        self.levels = rows.bit_length() - 1
        self.bits = all_levels - self.levels
        self.bands, self.halves = bands, halves
        self.parts = bands * halves
        self.own = rows // self.parts
        self.groups = groups if self.own % (SUB * groups) == 0 else 1
        self.per = self.own // self.groups
        self.blocks = span // LANES
        self.lead_blocks = cdiv(rows - 1, LANES)
        self.blocks_a = SUB - self.lead_blocks
        self.blocks_b = self.blocks - self.blocks_a
        self.pitch_a = SUB
        self.pitch_b = round_up(self.blocks_b + self.lead_blocks, SUB)
        self.total = self.blocks * halves
        reach = 2 ** (all_levels - 1)
        self.pitch_x = round_up(self.total + cdiv(reach, LANES) + 2, SUB)
        self.relays = RELAYS if self.groups > 1 and self.parts >= 2 * RELAYS else 0
        self.far = self.parts // 2
        starts = list(range(0, self.levels, 3))
        self.passes = [(first, min(3, self.levels - first)) for first in starts]
        assert rows <= 2 * LANES and 2 ** self.passes[-1][0] >= self.own
        self.window = max(rows, LANES)


def tree_kernel(plan, delays, spectra, *refs):
    p = plan
    G, parts, halves, bands = p.groups, p.parts, p.halves, p.bands
    refs = list(refs)

    def take(n):
        got = refs[:n]
        del refs[:n]
        return got

    outs, edges = take(G), take(G)
    relay = take(1)[0] if p.relays else None
    (rows_in, lead) = take(2)
    tree_a, tree_b = take(2), take(2)
    send_a = take(G)
    send_b = take(G)
    came_a = take(G)
    came_b = take(G)
    ready, ready_edge = take(G), take(G)
    buf_a, buf_b = take(2)
    own_delays, band_delays = take(2)
    sems, edge_sems, own_sems, in_sems, lead_sems, band_sems, relay_sems = take(7)

    beam, freq, tm = (lax.axis_index(n) for n in ("beam", "freq", "tm"))
    me = freq * halves + tm
    head = SUB * LANES

    load_a = pltpu.make_async_copy(spectra.at[:, :head], rows_in.at[:, :head], in_sems.at[0])
    load_b = pltpu.make_async_copy(spectra.at[:, head:], rows_in.at[:, head:], in_sems.at[1])
    own_first = freq * p.rows // p.window * p.window
    own_at = freq * p.rows - own_first
    load_own = pltpu.make_async_copy(
        delays.at[:, pl.ds(pl.multiple_of(own_first, LANES), p.window)], own_delays, in_sems.at[2]
    )
    load_bands = []
    for j in range(bands):
        at = (j * p.rows + me * p.own) // LANES * LANES
        load_bands.append(
            pltpu.make_async_copy(
                delays.at[:, pl.ds(pl.multiple_of(at, LANES), LANES)], band_delays.at[j], band_sems.at[j]
            )
        )
    load_a.start()
    load_own.start()
    load_b.start()
    for c in load_bands:
        c.start()

    def peer(k):
        other = flipped(me, k, parts)
        return other, (beam, other // halves, other % halves)

    barrier = pltpu.get_barrier_semaphore()
    for k in range(1, parts):
        pl.semaphore_signal(barrier, inc=1, device_id=peer(k)[1], device_id_type=MESH)

    def spread(buf, pitch, first, count, lead_count):
        def body(n, carry):
            at = pl.ds(pl.multiple_of(n * SUB, SUB), SUB)
            for b in range(count):
                v = rows_in[at, (first + b) * LANES : (first + b + 1) * LANES]
                buf[pl.ds(n * (SUB * pitch) + b, SUB, stride=pitch), :] = v
            for b in range(lead_count):
                v = lead[at, b * LANES : (b + 1) * LANES]
                v = jnp.where(tm < halves - 1, v, 0.0)
                buf[pl.ds(n * (SUB * pitch) + count + b, SUB, stride=pitch), :] = v
            return carry

        lax.fori_loop(0, p.rows // SUB, body, 0)

    def several(src, pitch, first, depth, base, put, only=None):
        lane = lax.broadcasted_iota(jnp.int32, (pitch, LANES), 1)
        half = 2**first
        rows = [src[pl.ds(pl.multiple_of((base + m * half) * pitch, SUB), pitch), :] for m in range(2**depth)]
        for t in range(depth):
            step = 2**t
            for m in range(2**depth):
                if m & step:
                    continue
                a, low = rows[m], rows[m + step]
                high = pltpu.roll(low, pitch - 1, 0)
                for q in (m, m + step):
                    if only is not None and q % 2 != only:
                        continue
                    shift = own_delays[first + t, own_at + base + q * half]
                    rows[q] = a + pltpu.roll(jnp.where(lane < shift, high, low), LANES - shift, 1)
        for m, v in enumerate(rows):
            if only is None or m % 2 == only:
                put(base + m * half, v)

    def levels(bufs, pitch, together, passes, only=None):
        src, dst = bufs
        for first, depth in passes:
            count = p.rows >> depth
            unroll = min(together, count)

            def body(n, carry, src=src, dst=dst, first=first, depth=depth, unroll=unroll):
                def put(row, v):
                    dst[pl.ds(pl.multiple_of(row * pitch, SUB), pitch), :] = v

                for u in range(unroll):
                    q = n * unroll + u
                    base = ((q >> first) << (first + depth)) + (q & (2**first - 1))
                    several(src, pitch, first, depth, base, put, only)
                return carry

            lax.fori_loop(0, count // unroll, body, 0)
            src, dst = dst, src
        return src

    def last_levels(src, pitch, out, blocks, group, per, together):
        first, depth = p.passes[-1]
        per_bits, own_bits = per.bit_length() - 1, p.own.bit_length() - 1
        count = (p.rows >> depth) * per // p.own
        unroll = min(together, count)

        def body(n, carry):
            for u in range(unroll):
                q = n * unroll + u
                base = ((q >> per_bits) << own_bits) + group * per + (q & (per - 1))
                at = (q & (per - 1)) * blocks

                def put(row, v):
                    out[row >> own_bits, pl.ds(at, blocks), :] = v[:blocks]

                several(src, pitch, first, depth, base, put)
            return carry

        lax.fori_loop(0, count // unroll, body, 0)

    def send(src, dst, turn, left_out=()):
        copies = []
        for k in range(parts - 1, 0, -1):
            if k in left_out:
                continue
            other, where = peer(k)
            c = pltpu.make_async_remote_copy(
                src_ref=src.at[other],
                dst_ref=dst.at[me],
                send_sem=sems.at[0, turn, k],
                recv_sem=sems.at[1, turn, k],
                device_id=where,
                device_id_type=MESH,
            )
            c.start()
            copies.append(c)
        c = pltpu.make_async_copy(src.at[me], dst.at[me], own_sems.at[turn])
        c.start()
        return copies, c

    def send_edges(src, dst, turn, left_out=()):
        copies = []
        for k in range(parts - 1, 0, -1):
            if k in left_out:
                continue
            other, where = peer(k)
            c = pltpu.make_async_remote_copy(
                src_ref=src.at[other],
                dst_ref=dst.at[me],
                send_sem=edge_sems.at[0, turn, k],
                recv_sem=edge_sems.at[1, turn, k],
                device_id=where,
                device_id_type=MESH,
            )

            @pl.when(other % halves < halves - 1)
            def _(c=c):
                c.start()

            copies.append((other, c))
        c = pltpu.make_async_copy(src.at[me], dst.at[me], own_sems.at[3 * G + turn])

        @pl.when(tm < halves - 1)
        def _(c=c):
            c.start()

        return copies, c

    def send_relays(src, src_edge):
        copies = []
        for k in range(p.relays):
            other, _ = peer(p.far + k)
            for n, (x, first, size) in enumerate(((src, 0, p.per * p.blocks), (src_edge, p.per * p.blocks, p.per))):
                to = relay.at[k, pl.ds(first, size)]
                if k == 0:
                    c = pltpu.make_async_copy(x.at[other], to, relay_sems.at[0, n, k])
                else:
                    c = pltpu.make_async_remote_copy(
                        src_ref=x.at[other],
                        dst_ref=to,
                        send_sem=relay_sems.at[0, n, k],
                        recv_sem=relay_sems.at[1, n, k],
                        device_id=peer(k)[1],
                        device_id_type=MESH,
                    )
                c.start()
                copies.append(c)
        return copies

    def arrive(sent):
        for c in sent[0]:
            c.wait_recv()
        sent[1].wait()

    load_a.wait()
    spread(tree_a[0], p.pitch_a, 0, SUB, 0)
    load_own.wait()
    sent_a = []
    split = p.passes[1][0] if len(p.passes) > 2 and G == 2 and p.per == 2 ** p.passes[1][0] else None
    src = levels(tree_a, p.pitch_a, 8, p.passes[:-1] if split is None else p.passes[:1])
    for g in range(G):
        ready_rows = src
        if split is not None:
            ready_rows = levels(tree_a[::-1], p.pitch_a, 8, p.passes[1:-1], g)
        last_levels(ready_rows, p.pitch_a, send_a[g], p.blocks_a, g, p.per, 8)
        if g == 0:
            pl.semaphore_wait(barrier, parts - 1)
        sent_a.append(send(send_a[g], came_a[g], g))

    left = (tm + halves - 1) % halves
    get_lead = pltpu.make_async_remote_copy(
        src_ref=spectra.at[:, : p.lead_blocks * LANES],
        dst_ref=lead,
        send_sem=lead_sems.at[0],
        recv_sem=lead_sems.at[1],
        device_id=(beam, freq, left),
        device_id_type=MESH,
    )
    get_lead.start()

    load_b.wait()
    get_lead.wait()
    spread(tree_b[0], p.pitch_b, p.blocks_a, p.blocks_b, p.lead_blocks)
    src = levels(tree_b, p.pitch_b, 4, p.passes[:-1])
    sent_b = []
    for g in range(G):
        last_levels(src, p.pitch_b, send_b[g], p.blocks_b, g, p.per, 4)
        sent_b.append(send(send_b[g], came_b[g], G + g))

    total, pitch, rows = p.total, p.pitch_x, p.per
    lane = lax.broadcasted_iota(jnp.int32, (total, LANES), 1)
    zero = jnp.zeros((pitch - total, LANES), jnp.float32)

    def clear(r, carry):
        for buf in (buf_a, buf_b):
            buf[pl.ds(r * pitch + total, pitch - total), :] = zero
        return carry

    lax.fori_loop(0, bands * rows, clear, 0)
    for buf in (buf_a, buf_b):
        buf[pl.ds(bands * rows * pitch, SUB), :] = jnp.zeros((SUB, LANES), jnp.float32)

    back, back_edges = [], []
    for c in load_bands:
        c.wait()
    for g in range(G):
        arrive(sent_a[g])
        arrive(sent_b[g])

        def gather(i, carry, g=g):
            for s in range(bands):
                at = (s * rows + i) * pitch
                for c in range(halves):
                    piece = came_a[g][s * halves + c, pl.ds(i * p.blocks_a, p.blocks_a), :]
                    buf_a[pl.ds(at + c * p.blocks, p.blocks_a), :] = piece
                    piece = came_b[g][s * halves + c, pl.ds(i * p.blocks_b, p.blocks_b), :]
                    buf_a[pl.ds(at + c * p.blocks + p.blocks_a, p.blocks_b), :] = piece
            return carry

        lax.fori_loop(0, rows, gather, 0)

        src, dst = buf_a, buf_b
        for level in range(p.bits):
            step = 2**level

            def one_row(i, carry, src=src, dst=dst, step=step, level=level, g=g):
                for j in range(bands):
                    base = (j // (2 * step)) * (2 * step) + j % step
                    at = (j * p.rows + me * p.own) % LANES + g * rows + i
                    shift = band_delays[j, p.levels + level, at]
                    at_a = pl.multiple_of((base * rows + i) * pitch, SUB)
                    at_b = pl.multiple_of(((base + step) * rows + i) * pitch, SUB)
                    if level < p.bits - 1:
                        a = src[pl.ds(at_a, total), :]
                        at = pl.multiple_of((j * rows + i) * pitch, SUB)
                        dst[pl.ds(at, total), :] = a + shifted(src, at_b, total, shift, lane)
                        continue
                    v = src[pl.ds(at_a, total), :] + shifted(src, at_b, total, shift, lane)
                    for c in range(halves):
                        first = c * p.blocks
                        ready[g][j * halves + c, pl.ds(i * p.blocks, p.blocks), :] = v[first : first + p.blocks]
                        if c > 0:
                            ready_edge[g][j * halves + c - 1, pl.ds(i, 1), :] = v[first : first + 1]
                return carry

            lax.fori_loop(0, rows, one_row, 0)
            src, dst = dst, src
        left_out = range(p.far, p.far + p.relays) if g == G - 1 else ()
        back.append(send(ready[g], outs[g], 2 * G + g, left_out))
        back_edges.append(send_edges(ready_edge[g], edges[g], g, left_out))
    relayed = send_relays(ready[G - 1], ready_edge[G - 1])
    for sent, (copies, c) in zip(back, back_edges):
        arrive(sent)

        @pl.when(tm < halves - 1)
        def _(copies=copies, c=c):
            for other, remote in copies:
                remote.wait_recv()
            c.wait()

    for c in relayed:
        c.wait()
    for sent in sent_a + sent_b + back:
        for c in sent[0]:
            c.wait_send()
    for copies, _ in back_edges:
        for other, remote in copies:

            @pl.when(other % halves < halves - 1)
            def _(remote=remote):
                remote.wait_send()


def dedisperse(p, delays, spectra):
    G, parts = p.groups, p.parts
    out_shape = jax.ShapeDtypeStruct((parts, p.per * p.blocks, LANES), jnp.float32)
    edge_shape = jax.ShapeDtypeStruct((parts, p.per, LANES), jnp.float32)
    relay_shapes = []
    if p.relays:
        relay_shapes = [jax.ShapeDtypeStruct((p.relays, p.per * (p.blocks + 1), LANES), jnp.float32)]
    here = pl.BlockSpec(memory_space=pl.ANY)
    f32 = jnp.float32
    turns = 3 * G
    return pl.pallas_call(
        functools.partial(tree_kernel, p),
        out_shape=[out_shape] * G + [edge_shape] * G + relay_shapes,
        in_specs=[pl.BlockSpec(memory_space=pltpu.MemorySpace.HBM)] * 2,
        out_specs=[here] * (2 * G + len(relay_shapes)),
        scratch_shapes=[
            pltpu.VMEM((p.rows, p.span), f32),
            pltpu.VMEM((p.rows, p.lead_blocks * LANES), f32),
        ]
        + [pltpu.VMEM((p.rows * p.pitch_a + SUB, LANES), f32)] * 2
        + [pltpu.VMEM((p.rows * p.pitch_b + SUB, LANES), f32)] * 2
        + [pltpu.VMEM((parts, p.per * p.blocks_a, LANES), f32)] * G
        + [pltpu.VMEM((parts, p.per * p.blocks_b, LANES), f32)] * G
        + [pltpu.VMEM((parts, p.per * p.blocks_a, LANES), f32)] * G
        + [pltpu.VMEM((parts, p.per * p.blocks_b, LANES), f32)] * G
        + [pltpu.VMEM((parts, p.per * p.blocks, LANES), f32)] * G
        + [pltpu.VMEM((parts, p.per, LANES), f32)] * G
        + [pltpu.VMEM((p.bands * p.per * p.pitch_x + SUB, LANES), f32)] * 2
        + [
            pltpu.SMEM((p.all_levels, p.window), jnp.int32),
            pltpu.SMEM((p.bands, p.all_levels, LANES), jnp.int32),
            pltpu.SemaphoreType.DMA((2, turns, parts)),
            pltpu.SemaphoreType.DMA((2, G, parts)),
            pltpu.SemaphoreType.DMA((turns + G,)),
            pltpu.SemaphoreType.DMA((3,)),
            pltpu.SemaphoreType.DMA((2,)),
            pltpu.SemaphoreType.DMA((p.bands,)),
            pltpu.SemaphoreType.DMA((2, 2, max(p.relays, 1))),
        ],
        compiler_params=pltpu.CompilerParams(
            collective_id=0, has_side_effects=True, vmem_limit_bytes=58 << 20
        ),
    )(delays, spectra)


def fill_matrix(matrix):
    source = lax.broadcasted_iota(jnp.int32, (LANES, LANES), 0)
    target = lax.broadcasted_iota(jnp.int32, (LANES, LANES), 1)
    for k, taken in enumerate((source <= target, source < LANES)):
        value = jnp.where(taken, 1.0, 0.0).astype(jnp.bfloat16)
        for n in range(2):
            matrix[n * LANES : (n + 1) * LANES, k * LANES : (k + 1) * LANES] = value


def prefix_sums(blocks, size, get, matrix, lhs, sums):
    for n in range(blocks + 1):
        v = get(n)
        h = v.astype(jnp.bfloat16)
        t = (v - h.astype(jnp.float32)).astype(jnp.bfloat16)
        lhs[n * size : (n + 1) * size, :LANES] = h
        lhs[n * size : (n + 1) * size, LANES:] = t
    sums[...] = jnp.dot(lhs[...], matrix[...], preferred_element_type=jnp.float32)


def box_ends(n, size, get, sums):
    low = sums[n * size : (n + 1) * size, :LANES]
    high = sums[n * size : (n + 1) * size, LANES:] + sums[(n + 1) * size : (n + 2) * size, :LANES]
    return low, high, low - get(n)


def box_scale(width, all_rows, shape):
    return 1.0 / jnp.sqrt(jnp.full(shape, width, jnp.int32).astype(jnp.float32) * all_rows)


def box(ends, width, scale, lane):
    low, high, before = ends
    shift = width - 1
    upto = pltpu.roll(jnp.where(lane < shift, high, low), LANES - shift, 1)
    return (upto - before) * scale


def filter_kernel(p, filters, parts, widths, *refs):
    G = p.groups
    xs, edges, (out, matrix, lhs, sums) = refs[:G], refs[G : 2 * G], refs[2 * G :]
    rows = parts * p.per
    size = G * rows
    last = lax.axis_index("tm") == p.halves - 1

    @pl.when(pl.program_id(0) == 0)
    def _():
        fill_matrix(matrix)

    def get(n):
        if n < p.blocks:
            return jnp.concatenate([x[pl.ds(n, rows, stride=p.blocks), :] for x in xs], axis=0)
        return jnp.where(last, 0.0, jnp.concatenate([e[...] for e in edges], axis=0))

    prefix_sums(p.blocks, size, get, matrix, lhs, sums)
    lane = lax.broadcasted_iota(jnp.int32, (size, LANES), 1)
    scale = [box_scale(widths[w], p.all_rows, (size, LANES)) for w in range(filters)]
    for n in range(p.blocks):
        ends = box_ends(n, size, get, sums)
        for w in range(filters):
            y = box(ends, widths[w], scale[w], lane)
            for g in range(G):
                shape = (out.shape[1], out.shape[2] // G, LANES)
                rows_out = slice(g * shape[1], (g + 1) * shape[1])
                out[w, :, rows_out, n * LANES : (n + 1) * LANES] = y[g * rows : (g + 1) * rows].reshape(shape)


def late_kernel(p, filters, widths, x, filtered, out, made, matrix, lhs, sums, sems):
    size = p.relays * p.per
    halves = p.halves
    tm = lax.axis_index("tm")
    me = lax.axis_index("freq") * halves + tm
    fill_matrix(matrix)
    stride = p.per * (p.blocks + 1)

    def get(n):
        pieces = []
        for k in range(p.relays):
            if n < p.blocks:
                v = x[pl.ds(k * stride + n, p.per, stride=p.blocks), :]
            else:
                v = jnp.where(tm == halves - 1, 0.0, x[pl.ds(k * stride + p.per * p.blocks, p.per), :])
            pieces.append(v)
        return jnp.concatenate(pieces, axis=0)

    prefix_sums(p.blocks, size, get, matrix, lhs, sums)
    lane = lax.broadcasted_iota(jnp.int32, (size, LANES), 1)
    copies = []
    for w in range(filters):
        scale = box_scale(widths[w], p.all_rows, (size, LANES))
        for n in range(p.blocks):
            y = box(box_ends(n, size, get, sums), widths[w], scale, lane)
            for k in range(p.relays):
                made[w, k, :, n * LANES : (n + 1) * LANES] = y[k * p.per : (k + 1) * p.per]
        for k in range(p.relays):
            part = flipped(me, p.far + k, p.parts)
            at = out.at[w, part, pl.ds((p.groups - 1) * p.per, p.per)]
            c = pltpu.make_async_copy(made.at[w, k], at, sems.at[w, k])
            c.start()
            copies.append(c)
    for c in copies:
        c.wait()


def filter_late(p, x, filtered, widths):
    filters = widths.shape[0]
    size = p.relays * p.per
    total = size * (p.blocks + 1)
    cells = filters * size * p.span
    return pl.pallas_call(
        functools.partial(late_kernel, p, filters),
        out_shape=jax.ShapeDtypeStruct(filtered.shape, jnp.float32),
        in_specs=[
            pl.BlockSpec(memory_space=SMEM),
            pl.BlockSpec(memory_space=VMEM),
            pl.BlockSpec(memory_space=pl.ANY),
        ],
        out_specs=pl.BlockSpec(memory_space=pl.ANY),
        scratch_shapes=[
            pltpu.VMEM((filters, p.relays, p.per, p.span), jnp.float32),
            pltpu.VMEM((2 * LANES, 2 * LANES), jnp.bfloat16),
            pltpu.VMEM((total, 2 * LANES), jnp.bfloat16),
            pltpu.VMEM((total, 2 * LANES), jnp.float32),
            pltpu.SemaphoreType.DMA((filters, p.relays)),
        ],
        input_output_aliases={2: 0},
        compiler_params=pltpu.CompilerParams(vmem_limit_bytes=32 << 20),
        cost_estimate=pl.CostEstimate(flops=96 * cells, bytes_accessed=4 * cells, transcendentals=0),
    )(widths, x, filtered)


def filter_rows(p, xs, edges, widths):
    filters = widths.shape[0]
    if p.per % SUB:
        parts, view = p.parts, (filters, 1, p.parts * p.own, p.span)
        block = view
    else:
        parts = PARTS if p.parts % PARTS == 0 else 1
        view = (filters, p.parts, p.own, p.span)
        block = (filters, parts, p.own, p.span)
    rows = parts * p.per
    total = rows * p.groups * (p.blocks + 1)
    cells = filters * p.rows * p.span
    return pl.pallas_call(
        functools.partial(filter_kernel, p, filters, parts),
        grid=(p.parts // parts,),
        out_shape=jax.ShapeDtypeStruct(view, jnp.float32),
        in_specs=[pl.BlockSpec(memory_space=SMEM)]
        + [pl.BlockSpec((rows * p.blocks, LANES), lambda s: (s, 0))] * p.groups
        + [pl.BlockSpec((rows, LANES), lambda s: (s, 0))] * p.groups,
        out_specs=pl.BlockSpec(block, lambda s: (0, s, 0, 0)),
        scratch_shapes=[
            pltpu.VMEM((2 * LANES, 2 * LANES), jnp.bfloat16),
            pltpu.VMEM((total, 2 * LANES), jnp.bfloat16),
            pltpu.VMEM((total, 2 * LANES), jnp.float32),
        ],
        compiler_params=pltpu.CompilerParams(vmem_limit_bytes=58 << 20),
        cost_estimate=pl.CostEstimate(flops=96 * cells, bytes_accessed=4 * cells, transcendentals=0),
    )(widths, *xs, *edges)


PARTS = 4
RELAYS = 4
GROUPS = 2


def local(spectra, delays, widths):
    rows, span = spectra.shape
    p = Plan(rows, span, *delays.shape, lax.axis_size("freq"), lax.axis_size("tm"), GROUPS)
    made = [x.reshape(-1, LANES) for x in dedisperse(p, delays, spectra)]
    xs, edges, relay = made[: p.groups], made[p.groups : 2 * p.groups], made[2 * p.groups :]
    if relay:
        swap = [(f, (f + p.bands // 2) % p.bands) for f in range(p.bands)]
        late = lax.ppermute(relay[0], "freq", swap)
    out = filter_rows(p, xs, edges, widths)
    if relay:
        out = filter_late(p, late, out, widths)
    return out.reshape(widths.shape[0], rows, span)


def solution(mesh):
    return jax.shard_map(
        local,
        mesh=mesh,
        in_specs=(P(("beam", "freq"), "tm"), P(), P()),
        out_specs=P(None, ("beam", "freq"), "tm"),
        check_vma=False,
    )
```

```python
import functools

import jax
import jax.numpy as jnp
from jax import lax
from jax.experimental import pallas as pl
from jax.experimental.pallas import tpu as pltpu
from jax.sharding import PartitionSpec as P

LANES = 128
SUB = 8
VMEM = pltpu.MemorySpace.VMEM
SMEM = pltpu.MemorySpace.SMEM
MESH = pl.DeviceIdType.MESH


def cdiv(a, b):
    return -(-a // b)


def round_up(a, b):
    return cdiv(a, b) * b


def shifted(src, start, width, shift, lane):
    start = start + lax.shift_right_logical(shift, LANES.bit_length() - 1)
    shift = shift & (LANES - 1)
    low = src[pl.ds(start, width), :]
    high = src[pl.ds(start + 1, width), :]
    return pltpu.roll(jnp.where(lane < shift, high, low), LANES - shift, 1)


def flipped(me, k, parts):
    other = me
    step = 1
    while step < parts:
        if k & step:
            other = other + step * (1 - 2 * ((me // step) % 2))
        step *= 2
    return other


class Plan:
    def __init__(self, rows, span, all_levels, all_rows, bands, halves, groups):
        self.rows, self.span = rows, span
        self.all_levels, self.all_rows = all_levels, all_rows
        self.levels = rows.bit_length() - 1
        self.bits = all_levels - self.levels
        self.bands, self.halves = bands, halves
        self.parts = bands * halves
        self.own = rows // self.parts
        self.groups = groups if self.own % (SUB * groups) == 0 else 1
        self.per = self.own // self.groups
        self.blocks = span // LANES
        self.lead_blocks = cdiv(rows - 1, LANES)
        self.blocks_a = SUB - self.lead_blocks
        self.blocks_b = self.blocks - self.blocks_a
        self.pitch_a = SUB
        self.pitch_b = round_up(self.blocks_b + self.lead_blocks, SUB)
        self.total = self.blocks * halves
        reach = 2 ** (all_levels - 1)
        self.pitch_x = round_up(self.total + cdiv(reach, LANES) + 2, SUB)
        self.late = LATE if self.groups > 1 and self.parts >= 16 else ()
        self.relays = [k for ks in self.late for k in ks]
        self.far = self.parts // 2
        starts = list(range(0, self.levels, 3))
        self.passes = [(first, min(3, self.levels - first)) for first in starts]
        assert rows <= 2 * LANES and 2 ** self.passes[-1][0] >= self.own
        self.window = max(rows, LANES)


def tree_kernel(plan, delays, spectra, *refs):
    p = plan
    G, parts, halves, bands = p.groups, p.parts, p.halves, p.bands
    refs = list(refs)

    def take(n):
        got = refs[:n]
        del refs[:n]
        return got

    outs, edges = take(G), take(G)
    relay = take(len(p.late))
    (rows_in, lead) = take(2)
    tree_a, tree_b = take(2), take(2)
    send_a = take(G)
    send_b = take(G)
    came_a = take(G)
    came_b = take(G)
    ready, ready_edge = take(G), take(G)
    buf_a, buf_b = take(2)
    own_delays, band_delays = take(2)
    sems, edge_sems, own_sems, in_sems, lead_sems, band_sems, relay_sems = take(7)

    beam, freq, tm = (lax.axis_index(n) for n in ("beam", "freq", "tm"))
    me = freq * halves + tm
    head = SUB * LANES

    load_a = pltpu.make_async_copy(spectra.at[:, :head], rows_in.at[:, :head], in_sems.at[0])
    load_b = pltpu.make_async_copy(spectra.at[:, head:], rows_in.at[:, head:], in_sems.at[1])
    own_first = freq * p.rows // p.window * p.window
    own_at = freq * p.rows - own_first
    load_own = pltpu.make_async_copy(
        delays.at[:, pl.ds(pl.multiple_of(own_first, LANES), p.window)], own_delays, in_sems.at[2]
    )
    load_bands = []
    for j in range(bands):
        at = (j * p.rows + me * p.own) // LANES * LANES
        load_bands.append(
            pltpu.make_async_copy(
                delays.at[:, pl.ds(pl.multiple_of(at, LANES), LANES)], band_delays.at[j], band_sems.at[j]
            )
        )
    load_own.start()
    load_a.start()
    load_b.start()
    for c in load_bands:
        c.start()

    def peer(k):
        other = flipped(me, k, parts)
        return other, (beam, other // halves, other % halves)

    barrier = pltpu.get_barrier_semaphore()
    for k in range(1, parts):
        pl.semaphore_signal(barrier, inc=1, device_id=peer(k)[1], device_id_type=MESH)

    def spread(buf, pitch, first, count, lead_count):
        def body(n, carry):
            for u in range(4):
                q = n * 4 + u
                at = pl.ds(pl.multiple_of(q * SUB, SUB), SUB)
                for b in range(count):
                    v = rows_in[at, (first + b) * LANES : (first + b + 1) * LANES]
                    buf[pl.ds(q * (SUB * pitch) + b, SUB, stride=pitch), :] = v
                for b in range(lead_count):
                    v = lead[at, b * LANES : (b + 1) * LANES]
                    v = jnp.where(tm < halves - 1, v, 0.0)
                    buf[pl.ds(q * (SUB * pitch) + count + b, SUB, stride=pitch), :] = v
            return carry

        lax.fori_loop(0, p.rows // SUB // 4, body, 0)

    def several(src, pitch, first, depth, base, put, only=None):
        lane = lax.broadcasted_iota(jnp.int32, (pitch, LANES), 1)
        half = 2**first
        rows = [src[pl.ds(pl.multiple_of((base + m * half) * pitch, SUB), pitch), :] for m in range(2**depth)]
        for t in range(depth):
            step = 2**t
            for m in range(2**depth):
                if m & step:
                    continue
                a, low = rows[m], rows[m + step]
                high = pltpu.roll(low, pitch - 1, 0)
                for q in (m, m + step):
                    if only is not None and q % 2 != only:
                        continue
                    shift = own_delays[first + t, own_at + base + q * half]
                    rows[q] = a + pltpu.roll(jnp.where(lane < shift, high, low), LANES - shift, 1)
        for m, v in enumerate(rows):
            if only is None or m % 2 == only:
                put(base + m * half, v)

    def levels(bufs, pitch, together, passes, only=None):
        src, dst = bufs
        for first, depth in passes:
            count = p.rows >> depth
            unroll = min(together, count)

            def body(n, carry, src=src, dst=dst, first=first, depth=depth, unroll=unroll):
                def put(row, v):
                    dst[pl.ds(pl.multiple_of(row * pitch, SUB), pitch), :] = v

                for u in range(unroll):
                    q = n * unroll + u
                    base = ((q >> first) << (first + depth)) + (q & (2**first - 1))
                    several(src, pitch, first, depth, base, put, only)
                return carry

            lax.fori_loop(0, count // unroll, body, 0)
            src, dst = dst, src
        return src

    def last_levels(src, pitch, out, blocks, group, per, together):
        first, depth = p.passes[-1]
        per_bits, own_bits = per.bit_length() - 1, p.own.bit_length() - 1
        count = (p.rows >> depth) * per // p.own
        unroll = min(together, count)

        def body(n, carry):
            for u in range(unroll):
                q = n * unroll + u
                base = ((q >> per_bits) << own_bits) + group * per + (q & (per - 1))
                at = (q & (per - 1)) * blocks

                def put(row, v):
                    out[row >> own_bits, pl.ds(at, blocks), :] = v[:blocks]

                several(src, pitch, first, depth, base, put)
            return carry

        lax.fori_loop(0, count // unroll, body, 0)

    def send(src, dst, turn, left_out=()):
        copies = []
        for k in range(parts - 1, 0, -1):
            if k in left_out:
                continue
            other, where = peer(k)
            c = pltpu.make_async_remote_copy(
                src_ref=src.at[other],
                dst_ref=dst.at[me],
                send_sem=sems.at[0, turn, k],
                recv_sem=sems.at[1, turn, k],
                device_id=where,
                device_id_type=MESH,
            )
            c.start()
            copies.append(c)
        c = pltpu.make_async_copy(src.at[me], dst.at[me], own_sems.at[turn])
        c.start()
        return copies, c

    def send_edges(src, dst, turn, left_out=()):
        copies = []
        for k in range(parts - 1, 0, -1):
            if k in left_out:
                continue
            other, where = peer(k)
            c = pltpu.make_async_remote_copy(
                src_ref=src.at[other],
                dst_ref=dst.at[me],
                send_sem=edge_sems.at[0, turn, k],
                recv_sem=edge_sems.at[1, turn, k],
                device_id=where,
                device_id_type=MESH,
            )

            @pl.when(other % halves < halves - 1)
            def _(c=c):
                c.start()

            copies.append((other, c))
        c = pltpu.make_async_copy(src.at[me], dst.at[me], own_sems.at[3 * G + turn])

        @pl.when(tm < halves - 1)
        def _(c=c):
            c.start()

        return copies, c

    def send_relays(src, src_edge):
        copies = []
        places = [x.at[n] for x, ks in zip(relay, p.late) for n in range(len(ks))]
        for slot, k in enumerate(p.relays):
            other, _ = peer(p.far + k)
            for n, (x, first, size) in enumerate(((src, 0, p.per * p.blocks), (src_edge, p.per * p.blocks, p.per))):
                to = places[slot].at[pl.ds(first, size)]
                if k == 0:
                    c = pltpu.make_async_copy(x.at[other], to, relay_sems.at[0, n, slot])
                else:
                    c = pltpu.make_async_remote_copy(
                        src_ref=x.at[other],
                        dst_ref=to,
                        send_sem=relay_sems.at[0, n, slot],
                        recv_sem=relay_sems.at[1, n, slot],
                        device_id=peer(k)[1],
                        device_id_type=MESH,
                    )
                c.start()
                copies.append(c)
        return copies

    def arrive(sent):
        for c in sent[0]:
            c.wait_recv()
        sent[1].wait()

    load_a.wait()
    spread(tree_a[0], p.pitch_a, 0, SUB, 0)
    load_own.wait()
    sent_a = []
    split = p.passes[1][0] if len(p.passes) > 2 and G == 2 and p.per == 2 ** p.passes[1][0] else None
    src = levels(tree_a, p.pitch_a, 8, p.passes[:-1] if split is None else p.passes[:1])
    for g in range(G):
        ready_rows = src
        if split is not None:
            ready_rows = levels(tree_a[::-1], p.pitch_a, 8, p.passes[1:-1], g)
        last_levels(ready_rows, p.pitch_a, send_a[g], p.blocks_a, g, p.per, 8)
        if g == 0:
            pl.semaphore_wait(barrier, parts - 1)
        sent_a.append(send(send_a[g], came_a[g], g))

    left = (tm + halves - 1) % halves
    get_lead = pltpu.make_async_remote_copy(
        src_ref=spectra.at[:, : p.lead_blocks * LANES],
        dst_ref=lead,
        send_sem=lead_sems.at[0],
        recv_sem=lead_sems.at[1],
        device_id=(beam, freq, left),
        device_id_type=MESH,
    )
    get_lead.start()

    load_b.wait()
    get_lead.wait()
    spread(tree_b[0], p.pitch_b, p.blocks_a, p.blocks_b, p.lead_blocks)
    src = levels(tree_b, p.pitch_b, 4, p.passes[:-1])
    sent_b = []
    for g in range(G):
        last_levels(src, p.pitch_b, send_b[g], p.blocks_b, g, p.per, 4)
        sent_b.append(send(send_b[g], came_b[g], G + g))

    total, pitch, rows = p.total, p.pitch_x, p.per
    lane = lax.broadcasted_iota(jnp.int32, (total, LANES), 1)
    zero = jnp.zeros((pitch - total, LANES), jnp.float32)

    def clear(r, carry):
        for buf in (buf_a, buf_b):
            buf[pl.ds(r * pitch + total, pitch - total), :] = zero
        return carry

    lax.fori_loop(0, bands * rows, clear, 0)
    for buf in (buf_a, buf_b):
        buf[pl.ds(bands * rows * pitch, SUB), :] = jnp.zeros((SUB, LANES), jnp.float32)

    back, back_edges = [], []
    for c in load_bands:
        c.wait()
    for g in range(G):
        arrive(sent_a[g])
        arrive(sent_b[g])

        def gather(i, carry, g=g):
            for s in range(bands):
                at = (s * rows + i) * pitch
                for c in range(halves):
                    piece = came_a[g][s * halves + c, pl.ds(i * p.blocks_a, p.blocks_a), :]
                    buf_a[pl.ds(at + c * p.blocks, p.blocks_a), :] = piece
                    piece = came_b[g][s * halves + c, pl.ds(i * p.blocks_b, p.blocks_b), :]
                    buf_a[pl.ds(at + c * p.blocks + p.blocks_a, p.blocks_b), :] = piece
            return carry

        lax.fori_loop(0, rows, gather, 0)

        src, dst = buf_a, buf_b
        for level in range(p.bits):
            step = 2**level

            def one_row(i, carry, src=src, dst=dst, step=step, level=level, g=g):
                for j in range(bands):
                    base = (j // (2 * step)) * (2 * step) + j % step
                    at = (j * p.rows + me * p.own) % LANES + g * rows + i
                    shift = band_delays[j, p.levels + level, at]
                    at_a = pl.multiple_of((base * rows + i) * pitch, SUB)
                    at_b = pl.multiple_of(((base + step) * rows + i) * pitch, SUB)
                    if level < p.bits - 1:
                        a = src[pl.ds(at_a, total), :]
                        at = pl.multiple_of((j * rows + i) * pitch, SUB)
                        dst[pl.ds(at, total), :] = a + shifted(src, at_b, total, shift, lane)
                        continue
                    v = src[pl.ds(at_a, total), :] + shifted(src, at_b, total, shift, lane)
                    for c in range(halves):
                        first = c * p.blocks
                        ready[g][j * halves + c, pl.ds(i * p.blocks, p.blocks), :] = v[first : first + p.blocks]
                        if c > 0:
                            ready_edge[g][j * halves + c - 1, pl.ds(i, 1), :] = v[first : first + 1]
                return carry

            lax.fori_loop(0, rows, one_row, 0)
            src, dst = dst, src
        left_out = [p.far + k for k in p.relays] if g == G - 1 else ()
        back.append(send(ready[g], outs[g], 2 * G + g, left_out))
        back_edges.append(send_edges(ready_edge[g], edges[g], g, left_out))
    relayed = send_relays(ready[G - 1], ready_edge[G - 1])
    for sent, (copies, c) in zip(back, back_edges):
        arrive(sent)

        @pl.when(tm < halves - 1)
        def _(copies=copies, c=c):
            for other, remote in copies:
                remote.wait_recv()
            c.wait()

    for c in relayed:
        c.wait()
    for sent in sent_a + sent_b + back:
        for c in sent[0]:
            c.wait_send()
    for copies, _ in back_edges:
        for other, remote in copies:

            @pl.when(other % halves < halves - 1)
            def _(remote=remote):
                remote.wait_send()


def dedisperse(p, delays, spectra):
    G, parts = p.groups, p.parts
    out_shape = jax.ShapeDtypeStruct((parts, p.per * p.blocks, LANES), jnp.float32)
    edge_shape = jax.ShapeDtypeStruct((parts, p.per, LANES), jnp.float32)
    relay_shapes = [
        jax.ShapeDtypeStruct((len(ks), p.per * (p.blocks + 1), LANES), jnp.float32) for ks in p.late
    ]
    here = pl.BlockSpec(memory_space=pl.ANY)
    f32 = jnp.float32
    turns = 3 * G
    return pl.pallas_call(
        functools.partial(tree_kernel, p),
        out_shape=[out_shape] * G + [edge_shape] * G + relay_shapes,
        in_specs=[pl.BlockSpec(memory_space=pltpu.MemorySpace.HBM)] * 2,
        out_specs=[here] * (2 * G + len(relay_shapes)),
        scratch_shapes=[
            pltpu.VMEM((p.rows, p.span), f32),
            pltpu.VMEM((p.rows, p.lead_blocks * LANES), f32),
        ]
        + [pltpu.VMEM((p.rows * p.pitch_a + SUB, LANES), f32)] * 2
        + [pltpu.VMEM((p.rows * p.pitch_b + SUB, LANES), f32)] * 2
        + [pltpu.VMEM((parts, p.per * p.blocks_a, LANES), f32)] * G
        + [pltpu.VMEM((parts, p.per * p.blocks_b, LANES), f32)] * G
        + [pltpu.VMEM((parts, p.per * p.blocks_a, LANES), f32)] * G
        + [pltpu.VMEM((parts, p.per * p.blocks_b, LANES), f32)] * G
        + [pltpu.VMEM((parts, p.per * p.blocks, LANES), f32)] * G
        + [pltpu.VMEM((parts, p.per, LANES), f32)] * G
        + [pltpu.VMEM((p.bands * p.per * p.pitch_x + SUB, LANES), f32)] * 2
        + [
            pltpu.SMEM((p.all_levels, p.window), jnp.int32),
            pltpu.SMEM((p.bands, p.all_levels, LANES), jnp.int32),
            pltpu.SemaphoreType.DMA((2, turns, parts)),
            pltpu.SemaphoreType.DMA((2, G, parts)),
            pltpu.SemaphoreType.DMA((turns + G,)),
            pltpu.SemaphoreType.DMA((3,)),
            pltpu.SemaphoreType.DMA((2,)),
            pltpu.SemaphoreType.DMA((p.bands,)),
            pltpu.SemaphoreType.DMA((2, 2, max(len(p.relays), 1))),
        ],
        compiler_params=pltpu.CompilerParams(
            collective_id=0, has_side_effects=True, vmem_limit_bytes=58 << 20
        ),
    )(delays, spectra)


def fill_matrix(matrix):
    source = lax.broadcasted_iota(jnp.int32, (LANES, LANES), 0)
    target = lax.broadcasted_iota(jnp.int32, (LANES, LANES), 1)
    for k, taken in enumerate((source <= target, source < LANES)):
        value = jnp.where(taken, 1.0, 0.0).astype(jnp.bfloat16)
        for n in range(2):
            matrix[n * LANES : (n + 1) * LANES, k * LANES : (k + 1) * LANES] = value


def prefix_sums(blocks, size, get, matrix, lhs, sums):
    for n in range(blocks + 1):
        v = get(n)
        h = v.astype(jnp.bfloat16)
        t = (v - h.astype(jnp.float32)).astype(jnp.bfloat16)
        lhs[n * size : (n + 1) * size, :LANES] = h
        lhs[n * size : (n + 1) * size, LANES:] = t
    used = slice(0, (blocks + 1) * size)
    sums[used, :] = jnp.dot(lhs[used, :], matrix[...], preferred_element_type=jnp.float32)


def box_ends(n, size, get, sums):
    low = sums[n * size : (n + 1) * size, :LANES]
    high = sums[n * size : (n + 1) * size, LANES:] + sums[(n + 1) * size : (n + 2) * size, :LANES]
    return low, high, low - get(n)


def box_scale(width, all_rows, shape):
    return 1.0 / jnp.sqrt(jnp.full(shape, width, jnp.int32).astype(jnp.float32) * all_rows)


def box(ends, width, scale, lane):
    low, high, before = ends
    shift = width - 1
    upto = pltpu.roll(jnp.where(lane < shift, high, low), LANES - shift, 1)
    return (upto - before) * scale


def filter_kernel(p, filters, parts, widths, *refs):
    G = p.groups
    xs, edges, (out, matrix, lhs, sums) = refs[:G], refs[G : 2 * G], refs[2 * G :]
    rows = parts * p.per
    tm = lax.axis_index("tm")
    me = lax.axis_index("freq") * p.halves + tm
    step = pl.program_id(0)

    @pl.when(step == 0)
    def _():
        fill_matrix(matrix)

    def run(groups):
        size = groups * rows

        def get(n):
            if n < p.blocks:
                pieces = [x[pl.ds(n, rows, stride=p.blocks), :] for x in xs[:groups]]
                return jnp.concatenate(pieces, axis=0)
            pieces = [e[...] for e in edges[:groups]]
            return jnp.where(tm == p.halves - 1, 0.0, jnp.concatenate(pieces, axis=0))

        prefix_sums(p.blocks, size, get, matrix, lhs, sums)
        lane = lax.broadcasted_iota(jnp.int32, (size, LANES), 1)
        scale = [box_scale(widths[w], p.all_rows, (size, LANES)) for w in range(filters)]
        for n in range(p.blocks):
            ends = box_ends(n, size, get, sums)
            for w in range(filters):
                y = box(ends, widths[w], scale[w], lane)
                for g in range(groups):
                    shape = (out.shape[1], out.shape[2] // G, LANES)
                    rows_out = slice(g * shape[1], (g + 1) * shape[1])
                    piece = y[g * rows : (g + 1) * rows].reshape(shape)
                    out[w, :, rows_out, n * LANES : (n + 1) * LANES] = piece

    if sorted(p.relays) != list(range(parts)):
        run(G)
        return
    late_step = flipped(me, p.far, p.parts) // parts

    @pl.when(step != late_step)
    def _():
        run(G)

    @pl.when(step == late_step)
    def _():
        run(G - 1)


def late_kernel(p, ks, filters, widths, x, filtered, out, made, matrix, lhs, sums, sems):
    size = len(ks) * p.per
    halves = p.halves
    tm = lax.axis_index("tm")
    me = lax.axis_index("freq") * halves + tm
    fill_matrix(matrix)
    stride = p.per * (p.blocks + 1)

    def get(n):
        pieces = []
        for k in range(len(ks)):
            if n < p.blocks:
                v = x[pl.ds(k * stride + n, p.per, stride=p.blocks), :]
            else:
                v = jnp.where(tm == halves - 1, 0.0, x[pl.ds(k * stride + p.per * p.blocks, p.per), :])
            pieces.append(v)
        return jnp.concatenate(pieces, axis=0)

    prefix_sums(p.blocks, size, get, matrix, lhs, sums)
    lane = lax.broadcasted_iota(jnp.int32, (size, LANES), 1)
    copies = []
    for w in range(filters):
        scale = box_scale(widths[w], p.all_rows, (size, LANES))
        for n in range(p.blocks):
            y = box(box_ends(n, size, get, sums), widths[w], scale, lane)
            for k in range(len(ks)):
                made[w, k, :, n * LANES : (n + 1) * LANES] = y[k * p.per : (k + 1) * p.per]
        for slot, k in enumerate(ks):
            part = flipped(me, p.far + k, p.parts)
            at = out.at[w, part, pl.ds((p.groups - 1) * p.per, p.per)]
            c = pltpu.make_async_copy(made.at[w, slot], at, sems.at[w, slot])
            c.start()
            copies.append(c)
    for c in copies:
        c.wait()


def filter_late(p, ks, x, filtered, widths):
    filters = widths.shape[0]
    size = len(ks) * p.per
    total = size * (p.blocks + 1)
    cells = filters * size * p.span
    return pl.pallas_call(
        functools.partial(late_kernel, p, ks, filters),
        out_shape=jax.ShapeDtypeStruct(filtered.shape, jnp.float32),
        in_specs=[
            pl.BlockSpec(memory_space=SMEM),
            pl.BlockSpec(memory_space=VMEM),
            pl.BlockSpec(memory_space=pl.ANY),
        ],
        out_specs=pl.BlockSpec(memory_space=pl.ANY),
        scratch_shapes=[
            pltpu.VMEM((filters, len(ks), p.per, p.span), jnp.float32),
            pltpu.VMEM((2 * LANES, 2 * LANES), jnp.bfloat16),
            pltpu.VMEM((total, 2 * LANES), jnp.bfloat16),
            pltpu.VMEM((total, 2 * LANES), jnp.float32),
            pltpu.SemaphoreType.DMA((filters, len(ks))),
        ],
        input_output_aliases={2: 0},
        compiler_params=pltpu.CompilerParams(vmem_limit_bytes=32 << 20),
        cost_estimate=pl.CostEstimate(flops=96 * cells, bytes_accessed=4 * cells, transcendentals=0),
    )(widths, x, filtered)


def filter_rows(p, xs, edges, widths):
    filters = widths.shape[0]
    if p.per % SUB:
        parts, view = p.parts, (filters, 1, p.parts * p.own, p.span)
        block = view
    else:
        parts = PARTS if p.parts % PARTS == 0 else 1
        view = (filters, p.parts, p.own, p.span)
        block = (filters, parts, p.own, p.span)
    rows = parts * p.per
    total = rows * p.groups * (p.blocks + 1)
    cells = filters * p.rows * p.span
    return pl.pallas_call(
        functools.partial(filter_kernel, p, filters, parts),
        grid=(p.parts // parts,),
        out_shape=jax.ShapeDtypeStruct(view, jnp.float32),
        in_specs=[pl.BlockSpec(memory_space=SMEM)]
        + [pl.BlockSpec((rows * p.blocks, LANES), lambda s: (s, 0))] * p.groups
        + [pl.BlockSpec((rows, LANES), lambda s: (s, 0))] * p.groups,
        out_specs=pl.BlockSpec(block, lambda s: (0, s, 0, 0)),
        scratch_shapes=[
            pltpu.VMEM((2 * LANES, 2 * LANES), jnp.bfloat16),
            pltpu.VMEM((total, 2 * LANES), jnp.bfloat16),
            pltpu.VMEM((total, 2 * LANES), jnp.float32),
        ],
        compiler_params=pltpu.CompilerParams(vmem_limit_bytes=58 << 20),
        cost_estimate=pl.CostEstimate(flops=96 * cells, bytes_accessed=4 * cells, transcendentals=0),
    )(widths, *xs, *edges)


PARTS = 4
LATE = ((0, 1), (2, 3))
GROUPS = 2


def local(spectra, delays, widths):
    rows, span = spectra.shape
    p = Plan(rows, span, *delays.shape, lax.axis_size("freq"), lax.axis_size("tm"), GROUPS)
    made = [x.reshape(-1, LANES) for x in dedisperse(p, delays, spectra)]
    xs, edges, relay = made[: p.groups], made[p.groups : 2 * p.groups], made[2 * p.groups :]
    swap = [(f, (f + p.bands // 2) % p.bands) for f in range(p.bands)]
    relay = [lax.ppermute(x, "freq", swap) for x in relay]
    out = filter_rows(p, xs, edges, widths)
    for ks, x in zip(p.late, relay):
        out = filter_late(p, ks, x, out, widths)
    return out.reshape(widths.shape[0], rows, span)


def solution(mesh):
    return jax.shard_map(
        local,
        mesh=mesh,
        in_specs=(P(("beam", "freq"), "tm"), P(), P()),
        out_specs=P(None, ("beam", "freq"), "tm"),
        check_vma=False,
    )
```

```python
import functools

import jax
import jax.numpy as jnp
from jax import lax
from jax.experimental import pallas as pl
from jax.experimental.pallas import tpu as pltpu
from jax.sharding import PartitionSpec as P

LANES = 128
SUB = 8
VMEM = pltpu.MemorySpace.VMEM
SMEM = pltpu.MemorySpace.SMEM
MESH = pl.DeviceIdType.MESH


def cdiv(a, b):
    return -(-a // b)


def round_up(a, b):
    return cdiv(a, b) * b


def shifted(src, start, width, shift, lane):
    start = start + lax.shift_right_logical(shift, LANES.bit_length() - 1)
    shift = shift & (LANES - 1)
    low = src[pl.ds(start, width), :]
    high = src[pl.ds(start + 1, width), :]
    return pltpu.roll(jnp.where(lane < shift, high, low), LANES - shift, 1)


def flipped(me, k, parts):
    other = me
    step = 1
    while step < parts:
        if k & step:
            other = other + step * (1 - 2 * ((me // step) % 2))
        step *= 2
    return other


class Plan:
    def __init__(self, rows, span, all_levels, all_rows, bands, halves, groups):
        self.rows, self.span = rows, span
        self.all_levels, self.all_rows = all_levels, all_rows
        self.levels = rows.bit_length() - 1
        self.bits = all_levels - self.levels
        self.bands, self.halves = bands, halves
        self.parts = bands * halves
        self.own = rows // self.parts
        self.groups = groups if self.own % (SUB * groups) == 0 else 1
        self.per = self.own // self.groups
        self.blocks = span // LANES
        self.lead_blocks = cdiv(rows - 1, LANES)
        self.blocks_a = SUB - self.lead_blocks
        self.blocks_b = self.blocks - self.blocks_a
        self.pitch_a = SUB
        self.pitch_b = round_up(self.blocks_b + self.lead_blocks, SUB)
        self.total = self.blocks * halves
        reach = 2 ** (all_levels - 1)
        self.pitch_x = round_up(self.total + cdiv(reach, LANES) + 2, SUB)
        self.relays = RELAYS if self.groups > 1 and self.parts >= 2 * RELAYS else 0
        self.far = self.parts // 2
        starts = list(range(0, self.levels, 3))
        self.passes = [(first, min(3, self.levels - first)) for first in starts]
        assert rows <= 2 * LANES and 2 ** self.passes[-1][0] >= self.own
        self.window = max(rows, LANES)


def tree_kernel(plan, delays, spectra, *refs):
    p = plan
    G, parts, halves, bands = p.groups, p.parts, p.halves, p.bands
    refs = list(refs)

    def take(n):
        got = refs[:n]
        del refs[:n]
        return got

    outs, edges = take(G), take(G)
    relay = take(1)[0] if p.relays else None
    (rows_in, lead) = take(2)
    tree_a, tree_b = take(2), take(2)
    send_a = take(G)
    send_b = take(G)
    came_a = take(G)
    came_b = take(G)
    ready, ready_edge = take(G), take(G)
    buf_a, buf_b = take(2)
    own_delays, band_delays = take(2)
    sems, edge_sems, own_sems, in_sems, lead_sems, band_sems, relay_sems = take(7)

    beam, freq, tm = (lax.axis_index(n) for n in ("beam", "freq", "tm"))
    me = freq * halves + tm
    head = SUB * LANES

    load_a = pltpu.make_async_copy(spectra.at[:, :head], rows_in.at[:, :head], in_sems.at[0])
    load_b = pltpu.make_async_copy(spectra.at[:, head:], rows_in.at[:, head:], in_sems.at[1])
    own_first = freq * p.rows // p.window * p.window
    own_at = freq * p.rows - own_first
    load_own = pltpu.make_async_copy(
        delays.at[:, pl.ds(pl.multiple_of(own_first, LANES), p.window)], own_delays, in_sems.at[2]
    )
    load_bands = []
    for j in range(bands):
        at = (j * p.rows + me * p.own) // LANES * LANES
        load_bands.append(
            pltpu.make_async_copy(
                delays.at[:, pl.ds(pl.multiple_of(at, LANES), LANES)], band_delays.at[j], band_sems.at[j]
            )
        )
    load_own.start()
    load_a.start()
    load_b.start()
    for c in load_bands:
        c.start()

    def peer(k):
        other = flipped(me, k, parts)
        return other, (beam, other // halves, other % halves)

    barrier = pltpu.get_barrier_semaphore()
    for k in range(1, parts):
        pl.semaphore_signal(barrier, inc=1, device_id=peer(k)[1], device_id_type=MESH)

    def spread(buf, pitch, first, count, lead_count):
        def body(n, carry):
            for u in range(4):
                q = n * 4 + u
                at = pl.ds(pl.multiple_of(q * SUB, SUB), SUB)
                for b in range(count):
                    v = rows_in[at, (first + b) * LANES : (first + b + 1) * LANES]
                    buf[pl.ds(q * (SUB * pitch) + b, SUB, stride=pitch), :] = v
                for b in range(lead_count):
                    v = lead[at, b * LANES : (b + 1) * LANES]
                    v = jnp.where(tm < halves - 1, v, 0.0)
                    buf[pl.ds(q * (SUB * pitch) + count + b, SUB, stride=pitch), :] = v
            return carry

        lax.fori_loop(0, p.rows // SUB // 4, body, 0)

    def several(src, pitch, first, depth, base, put, only=None):
        lane = lax.broadcasted_iota(jnp.int32, (pitch, LANES), 1)
        half = 2**first
        rows = [src[pl.ds(pl.multiple_of((base + m * half) * pitch, SUB), pitch), :] for m in range(2**depth)]
        for t in range(depth):
            step = 2**t
            for m in range(2**depth):
                if m & step:
                    continue
                a, low = rows[m], rows[m + step]
                high = pltpu.roll(low, pitch - 1, 0)
                for q in (m, m + step):
                    if only is not None and q % 2 != only:
                        continue
                    shift = own_delays[first + t, own_at + base + q * half]
                    rows[q] = a + pltpu.roll(jnp.where(lane < shift, high, low), LANES - shift, 1)
        for m, v in enumerate(rows):
            if only is None or m % 2 == only:
                put(base + m * half, v)

    def levels(bufs, pitch, together, passes, only=None):
        src, dst = bufs
        for first, depth in passes:
            count = p.rows >> depth
            unroll = min(together, count)

            def body(n, carry, src=src, dst=dst, first=first, depth=depth, unroll=unroll):
                def put(row, v):
                    dst[pl.ds(pl.multiple_of(row * pitch, SUB), pitch), :] = v

                for u in range(unroll):
                    q = n * unroll + u
                    base = ((q >> first) << (first + depth)) + (q & (2**first - 1))
                    several(src, pitch, first, depth, base, put, only)
                return carry

            lax.fori_loop(0, count // unroll, body, 0)
            src, dst = dst, src
        return src

    def last_levels(src, pitch, out, blocks, group, per, together):
        first, depth = p.passes[-1]
        per_bits, own_bits = per.bit_length() - 1, p.own.bit_length() - 1
        count = (p.rows >> depth) * per // p.own
        unroll = min(together, count)

        def body(n, carry):
            for u in range(unroll):
                q = n * unroll + u
                base = ((q >> per_bits) << own_bits) + group * per + (q & (per - 1))
                at = (q & (per - 1)) * blocks

                def put(row, v):
                    out[row >> own_bits, pl.ds(at, blocks), :] = v[:blocks]

                several(src, pitch, first, depth, base, put)
            return carry

        lax.fori_loop(0, count // unroll, body, 0)

    def send(src, dst, turn, left_out=()):
        copies = []
        for k in range(parts - 1, 0, -1):
            if k in left_out:
                continue
            other, where = peer(k)
            c = pltpu.make_async_remote_copy(
                src_ref=src.at[other],
                dst_ref=dst.at[me],
                send_sem=sems.at[0, turn, k],
                recv_sem=sems.at[1, turn, k],
                device_id=where,
                device_id_type=MESH,
            )
            c.start()
            copies.append(c)
        c = pltpu.make_async_copy(src.at[me], dst.at[me], own_sems.at[turn])
        c.start()
        return copies, c

    def send_edges(src, dst, turn, left_out=()):
        copies = []
        for k in range(parts - 1, 0, -1):
            if k in left_out:
                continue
            other, where = peer(k)
            c = pltpu.make_async_remote_copy(
                src_ref=src.at[other],
                dst_ref=dst.at[me],
                send_sem=edge_sems.at[0, turn, k],
                recv_sem=edge_sems.at[1, turn, k],
                device_id=where,
                device_id_type=MESH,
            )

            @pl.when(other % halves < halves - 1)
            def _(c=c):
                c.start()

            copies.append((other, c))
        c = pltpu.make_async_copy(src.at[me], dst.at[me], own_sems.at[3 * G + turn])

        @pl.when(tm < halves - 1)
        def _(c=c):
            c.start()

        return copies, c

    def send_relays(src, src_edge):
        copies = []
        for k in range(p.relays):
            other, _ = peer(p.far + k)
            for n, (x, first, size) in enumerate(((src, 0, p.per * p.blocks), (src_edge, p.per * p.blocks, p.per))):
                to = relay.at[k, pl.ds(first, size)]
                if k == 0:
                    c = pltpu.make_async_copy(x.at[other], to, relay_sems.at[0, n, k])
                else:
                    c = pltpu.make_async_remote_copy(
                        src_ref=x.at[other],
                        dst_ref=to,
                        send_sem=relay_sems.at[0, n, k],
                        recv_sem=relay_sems.at[1, n, k],
                        device_id=peer(k)[1],
                        device_id_type=MESH,
                    )
                c.start()
                copies.append(c)
        return copies

    def arrive(sent):
        for c in sent[0]:
            c.wait_recv()
        sent[1].wait()

    load_a.wait()
    spread(tree_a[0], p.pitch_a, 0, SUB, 0)
    load_own.wait()
    sent_a = []
    split = p.passes[1][0] if len(p.passes) > 2 and G == 2 and p.per == 2 ** p.passes[1][0] else None
    src = levels(tree_a, p.pitch_a, 8, p.passes[:-1] if split is None else p.passes[:1])
    for g in range(G):
        ready_rows = src
        if split is not None:
            ready_rows = levels(tree_a[::-1], p.pitch_a, 8, p.passes[1:-1], g)
        last_levels(ready_rows, p.pitch_a, send_a[g], p.blocks_a, g, p.per, 8)
        if g == 0:
            pl.semaphore_wait(barrier, parts - 1)
        sent_a.append(send(send_a[g], came_a[g], g))

    left = (tm + halves - 1) % halves
    get_lead = pltpu.make_async_remote_copy(
        src_ref=spectra.at[:, : p.lead_blocks * LANES],
        dst_ref=lead,
        send_sem=lead_sems.at[0],
        recv_sem=lead_sems.at[1],
        device_id=(beam, freq, left),
        device_id_type=MESH,
    )
    get_lead.start()

    load_b.wait()
    get_lead.wait()
    spread(tree_b[0], p.pitch_b, p.blocks_a, p.blocks_b, p.lead_blocks)
    src = levels(tree_b, p.pitch_b, 4, p.passes[:-1])
    sent_b = []
    for g in range(G):
        last_levels(src, p.pitch_b, send_b[g], p.blocks_b, g, p.per, 4)
        sent_b.append(send(send_b[g], came_b[g], G + g))

    total, pitch, rows = p.total, p.pitch_x, p.per
    lane = lax.broadcasted_iota(jnp.int32, (total, LANES), 1)
    zero = jnp.zeros((pitch - total, LANES), jnp.float32)

    def clear(r, carry):
        for buf in (buf_a, buf_b):
            buf[pl.ds(r * pitch + total, pitch - total), :] = zero
        return carry

    lax.fori_loop(0, bands * rows, clear, 0)
    for buf in (buf_a, buf_b):
        buf[pl.ds(bands * rows * pitch, SUB), :] = jnp.zeros((SUB, LANES), jnp.float32)

    back, back_edges = [], []
    for c in load_bands:
        c.wait()
    for g in range(G):
        arrive(sent_a[g])
        arrive(sent_b[g])

        def gather(i, carry, g=g):
            for s in range(bands):
                at = (s * rows + i) * pitch
                for c in range(halves):
                    piece = came_a[g][s * halves + c, pl.ds(i * p.blocks_a, p.blocks_a), :]
                    buf_a[pl.ds(at + c * p.blocks, p.blocks_a), :] = piece
                    piece = came_b[g][s * halves + c, pl.ds(i * p.blocks_b, p.blocks_b), :]
                    buf_a[pl.ds(at + c * p.blocks + p.blocks_a, p.blocks_b), :] = piece
            return carry

        lax.fori_loop(0, rows, gather, 0)

        src, dst = buf_a, buf_b
        for level in range(p.bits):
            step = 2**level

            def one_row(i, carry, src=src, dst=dst, step=step, level=level, g=g):
                for j in range(bands):
                    base = (j // (2 * step)) * (2 * step) + j % step
                    at = (j * p.rows + me * p.own) % LANES + g * rows + i
                    shift = band_delays[j, p.levels + level, at]
                    at_a = pl.multiple_of((base * rows + i) * pitch, SUB)
                    at_b = pl.multiple_of(((base + step) * rows + i) * pitch, SUB)
                    if level < p.bits - 1:
                        a = src[pl.ds(at_a, total), :]
                        at = pl.multiple_of((j * rows + i) * pitch, SUB)
                        dst[pl.ds(at, total), :] = a + shifted(src, at_b, total, shift, lane)
                        continue
                    v = src[pl.ds(at_a, total), :] + shifted(src, at_b, total, shift, lane)
                    for c in range(halves):
                        first = c * p.blocks
                        ready[g][j * halves + c, pl.ds(i * p.blocks, p.blocks), :] = v[first : first + p.blocks]
                        if c > 0:
                            ready_edge[g][j * halves + c - 1, pl.ds(i, 1), :] = v[first : first + 1]
                return carry

            lax.fori_loop(0, rows, one_row, 0)
            src, dst = dst, src
        left_out = range(p.far, p.far + p.relays) if g == G - 1 else ()
        back.append(send(ready[g], outs[g], 2 * G + g, left_out))
        back_edges.append(send_edges(ready_edge[g], edges[g], g, left_out))
    relayed = send_relays(ready[G - 1], ready_edge[G - 1])
    for sent, (copies, c) in zip(back, back_edges):
        arrive(sent)

        @pl.when(tm < halves - 1)
        def _(copies=copies, c=c):
            for other, remote in copies:
                remote.wait_recv()
            c.wait()

    for c in relayed:
        c.wait()
    for sent in sent_a + sent_b + back:
        for c in sent[0]:
            c.wait_send()
    for copies, _ in back_edges:
        for other, remote in copies:

            @pl.when(other % halves < halves - 1)
            def _(remote=remote):
                remote.wait_send()


def dedisperse(p, delays, spectra):
    G, parts = p.groups, p.parts
    out_shape = jax.ShapeDtypeStruct((parts, p.per * p.blocks, LANES), jnp.float32)
    edge_shape = jax.ShapeDtypeStruct((parts, p.per, LANES), jnp.float32)
    relay_shapes = []
    if p.relays:
        relay_shapes = [jax.ShapeDtypeStruct((p.relays, p.per * (p.blocks + 1), LANES), jnp.float32)]
    here = pl.BlockSpec(memory_space=pl.ANY)
    f32 = jnp.float32
    turns = 3 * G
    return pl.pallas_call(
        functools.partial(tree_kernel, p),
        out_shape=[out_shape] * G + [edge_shape] * G + relay_shapes,
        in_specs=[pl.BlockSpec(memory_space=pltpu.MemorySpace.HBM)] * 2,
        out_specs=[here] * (2 * G + len(relay_shapes)),
        scratch_shapes=[
            pltpu.VMEM((p.rows, p.span), f32),
            pltpu.VMEM((p.rows, p.lead_blocks * LANES), f32),
        ]
        + [pltpu.VMEM((p.rows * p.pitch_a + SUB, LANES), f32)] * 2
        + [pltpu.VMEM((p.rows * p.pitch_b + SUB, LANES), f32)] * 2
        + [pltpu.VMEM((parts, p.per * p.blocks_a, LANES), f32)] * G
        + [pltpu.VMEM((parts, p.per * p.blocks_b, LANES), f32)] * G
        + [pltpu.VMEM((parts, p.per * p.blocks_a, LANES), f32)] * G
        + [pltpu.VMEM((parts, p.per * p.blocks_b, LANES), f32)] * G
        + [pltpu.VMEM((parts, p.per * p.blocks, LANES), f32)] * G
        + [pltpu.VMEM((parts, p.per, LANES), f32)] * G
        + [pltpu.VMEM((p.bands * p.per * p.pitch_x + SUB, LANES), f32)] * 2
        + [
            pltpu.SMEM((p.all_levels, p.window), jnp.int32),
            pltpu.SMEM((p.bands, p.all_levels, LANES), jnp.int32),
            pltpu.SemaphoreType.DMA((2, turns, parts)),
            pltpu.SemaphoreType.DMA((2, G, parts)),
            pltpu.SemaphoreType.DMA((turns + G,)),
            pltpu.SemaphoreType.DMA((3,)),
            pltpu.SemaphoreType.DMA((2,)),
            pltpu.SemaphoreType.DMA((p.bands,)),
            pltpu.SemaphoreType.DMA((2, 2, max(p.relays, 1))),
        ],
        compiler_params=pltpu.CompilerParams(
            collective_id=0, has_side_effects=True, vmem_limit_bytes=58 << 20
        ),
    )(delays, spectra)


def fill_matrix(matrix):
    source = lax.broadcasted_iota(jnp.int32, (LANES, LANES), 0)
    target = lax.broadcasted_iota(jnp.int32, (LANES, LANES), 1)
    for k, taken in enumerate((source <= target, source < LANES)):
        value = jnp.where(taken, 1.0, 0.0).astype(jnp.bfloat16)
        for n in range(2):
            matrix[n * LANES : (n + 1) * LANES, k * LANES : (k + 1) * LANES] = value


def prefix_sums(blocks, size, get, matrix, lhs, sums):
    for n in range(blocks + 1):
        v = get(n)
        h = v.astype(jnp.bfloat16)
        t = (v - h.astype(jnp.float32)).astype(jnp.bfloat16)
        lhs[n * size : (n + 1) * size, :LANES] = h
        lhs[n * size : (n + 1) * size, LANES:] = t
    sums[...] = jnp.dot(lhs[...], matrix[...], preferred_element_type=jnp.float32)


def box_ends(n, size, get, sums):
    low = sums[n * size : (n + 1) * size, :LANES]
    high = sums[n * size : (n + 1) * size, LANES:] + sums[(n + 1) * size : (n + 2) * size, :LANES]
    return low, high, low - get(n)


def box_scale(width, all_rows, shape):
    return 1.0 / jnp.sqrt(jnp.full(shape, width, jnp.int32).astype(jnp.float32) * all_rows)


def box(ends, width, scale, lane):
    low, high, before = ends
    shift = width - 1
    upto = pltpu.roll(jnp.where(lane < shift, high, low), LANES - shift, 1)
    return (upto - before) * scale


def filter_kernel(p, filters, parts, widths, *refs):
    G = p.groups
    xs, edges, (out, matrix, lhs, sums) = refs[:G], refs[G : 2 * G], refs[2 * G :]
    rows = parts * p.per
    size = G * rows
    last = lax.axis_index("tm") == p.halves - 1

    @pl.when(pl.program_id(0) == 0)
    def _():
        fill_matrix(matrix)

    def get(n):
        if n < p.blocks:
            return jnp.concatenate([x[pl.ds(n, rows, stride=p.blocks), :] for x in xs], axis=0)
        return jnp.where(last, 0.0, jnp.concatenate([e[...] for e in edges], axis=0))

    prefix_sums(p.blocks, size, get, matrix, lhs, sums)
    lane = lax.broadcasted_iota(jnp.int32, (size, LANES), 1)
    scale = [box_scale(widths[w], p.all_rows, (size, LANES)) for w in range(filters)]
    for n in range(p.blocks):
        ends = box_ends(n, size, get, sums)
        for w in range(filters):
            y = box(ends, widths[w], scale[w], lane)
            for g in range(G):
                shape = (out.shape[1], out.shape[2] // G, LANES)
                rows_out = slice(g * shape[1], (g + 1) * shape[1])
                out[w, :, rows_out, n * LANES : (n + 1) * LANES] = y[g * rows : (g + 1) * rows].reshape(shape)


def late_kernel(p, filters, widths, x, filtered, out, made, matrix, lhs, sums, sems):
    size = p.relays * p.per
    halves = p.halves
    tm = lax.axis_index("tm")
    me = lax.axis_index("freq") * halves + tm
    fill_matrix(matrix)
    stride = p.per * (p.blocks + 1)

    def get(n):
        pieces = []
        for k in range(p.relays):
            if n < p.blocks:
                v = x[pl.ds(k * stride + n, p.per, stride=p.blocks), :]
            else:
                v = jnp.where(tm == halves - 1, 0.0, x[pl.ds(k * stride + p.per * p.blocks, p.per), :])
            pieces.append(v)
        return jnp.concatenate(pieces, axis=0)

    prefix_sums(p.blocks, size, get, matrix, lhs, sums)
    lane = lax.broadcasted_iota(jnp.int32, (size, LANES), 1)
    copies = []
    for w in range(filters):
        scale = box_scale(widths[w], p.all_rows, (size, LANES))
        for n in range(p.blocks):
            y = box(box_ends(n, size, get, sums), widths[w], scale, lane)
            for k in range(p.relays):
                made[w, k, :, n * LANES : (n + 1) * LANES] = y[k * p.per : (k + 1) * p.per]
        for k in range(p.relays):
            part = flipped(me, p.far + k, p.parts)
            at = out.at[w, part, pl.ds((p.groups - 1) * p.per, p.per)]
            c = pltpu.make_async_copy(made.at[w, k], at, sems.at[w, k])
            c.start()
            copies.append(c)
    for c in copies:
        c.wait()


def filter_late(p, x, filtered, widths):
    filters = widths.shape[0]
    size = p.relays * p.per
    total = size * (p.blocks + 1)
    cells = filters * size * p.span
    return pl.pallas_call(
        functools.partial(late_kernel, p, filters),
        out_shape=jax.ShapeDtypeStruct(filtered.shape, jnp.float32),
        in_specs=[
            pl.BlockSpec(memory_space=SMEM),
            pl.BlockSpec(memory_space=VMEM),
            pl.BlockSpec(memory_space=pl.ANY),
        ],
        out_specs=pl.BlockSpec(memory_space=pl.ANY),
        scratch_shapes=[
            pltpu.VMEM((filters, p.relays, p.per, p.span), jnp.float32),
            pltpu.VMEM((2 * LANES, 2 * LANES), jnp.bfloat16),
            pltpu.VMEM((total, 2 * LANES), jnp.bfloat16),
            pltpu.VMEM((total, 2 * LANES), jnp.float32),
            pltpu.SemaphoreType.DMA((filters, p.relays)),
        ],
        input_output_aliases={2: 0},
        compiler_params=pltpu.CompilerParams(vmem_limit_bytes=32 << 20),
        cost_estimate=pl.CostEstimate(flops=96 * cells, bytes_accessed=4 * cells, transcendentals=0),
    )(widths, x, filtered)


def filter_rows(p, xs, edges, widths):
    filters = widths.shape[0]
    if p.per % SUB:
        parts, view = p.parts, (filters, 1, p.parts * p.own, p.span)
        block = view
    else:
        parts = PARTS if p.parts % PARTS == 0 else 1
        view = (filters, p.parts, p.own, p.span)
        block = (filters, parts, p.own, p.span)
    rows = parts * p.per
    total = rows * p.groups * (p.blocks + 1)
    cells = filters * p.rows * p.span
    return pl.pallas_call(
        functools.partial(filter_kernel, p, filters, parts),
        grid=(p.parts // parts,),
        out_shape=jax.ShapeDtypeStruct(view, jnp.float32),
        in_specs=[pl.BlockSpec(memory_space=SMEM)]
        + [pl.BlockSpec((rows * p.blocks, LANES), lambda s: (s, 0))] * p.groups
        + [pl.BlockSpec((rows, LANES), lambda s: (s, 0))] * p.groups,
        out_specs=pl.BlockSpec(block, lambda s: (0, s, 0, 0)),
        scratch_shapes=[
            pltpu.VMEM((2 * LANES, 2 * LANES), jnp.bfloat16),
            pltpu.VMEM((total, 2 * LANES), jnp.bfloat16),
            pltpu.VMEM((total, 2 * LANES), jnp.float32),
        ],
        compiler_params=pltpu.CompilerParams(vmem_limit_bytes=58 << 20),
        cost_estimate=pl.CostEstimate(flops=96 * cells, bytes_accessed=4 * cells, transcendentals=0),
    )(widths, *xs, *edges)


PARTS = 4
RELAYS = 4
GROUPS = 2


def local(spectra, delays, widths):
    rows, span = spectra.shape
    p = Plan(rows, span, *delays.shape, lax.axis_size("freq"), lax.axis_size("tm"), GROUPS)
    made = [x.reshape(-1, LANES) for x in dedisperse(p, delays, spectra)]
    xs, edges, relay = made[: p.groups], made[p.groups : 2 * p.groups], made[2 * p.groups :]
    if relay:
        swap = [(f, (f + p.bands // 2) % p.bands) for f in range(p.bands)]
        late = lax.ppermute(relay[0], "freq", swap)
    out = filter_rows(p, xs, edges, widths)
    if relay:
        out = filter_late(p, late, out, widths)
    return out.reshape(widths.shape[0], rows, span)


def solution(mesh):
    return jax.shard_map(
        local,
        mesh=mesh,
        in_specs=(P(("beam", "freq"), "tm"), P(), P()),
        out_specs=P(None, ("beam", "freq"), "tm"),
        check_vma=False,
    )
```
